512 devices in a mesh: gx: 8 (over z_hi, x), gy: 8 (over y, core), ta: 8 (over z_lo).
Axes of the slice: x: 4, y: 4, z: 16 (z_hi: 2, z_lo: 8; z = z_hi * 8 + z_lo), core: 2. Of those that a mesh axis runs over, the one named last changes fastest.
Arguments:
- frames: bfloat16 [64, 64, 512, 128], P('ta', 'gx', 'gy'), may hold values from -6 to 6
- in_weight: bfloat16 [3, 3, 128, 128], replicated, may hold values from -0.1875 to 0.1875
- out_weight: bfloat16 [3, 3, 128, 128], replicated, may hold values from -0.1875 to 0.1875
- decays: float32 [64, 128], P('ta'), may hold values from 0.05 to 0.999, as said below
Outputs:
- mixed_frames: bfloat16 [64, 64, 512, 128], P('ta', 'gx', 'gy')
The draws below stay inside these ranges and needn't reach their ends.
Inputs may be any that keep to these rules, and one draw needn't show every extreme that they name: `decays`: every factor lies strictly between 0 and 1.
All inputs are finite; a program needn't handle non-finite values.
Results may differ from the reference program's by a relative error of at most 0.0031.
Values may be sent and summed in bfloat16 or wider, within the bound.
A program may use at most 64 MiB of HBM per device.

```python
import math
import jax
import jax.numpy as jnp
from jax import lax

FEAT = 128
LATENT_FEATURES = 128
SEQUENCE_LENGTH = 64
HEIGHT = 64
WIDTH = 512


def draw_decays(key, part):
    generator_seeds = jax.random.split(jax.random.fold_in(key, 11), 6)
    share = 0.5
    quick = jax.random.uniform(generator_seeds[0], (LATENT_FEATURES,)) < share
    quick_rate = jax.random.uniform(generator_seeds[1], (LATENT_FEATURES,), jnp.float32, 0.2, 0.6)
    slow_rate = jnp.exp(-jax.random.uniform(generator_seeds[2], (LATENT_FEATURES,), jnp.float32, 0.05, 0.4) * math.log(10.0) / SEQUENCE_LENGTH)
    nominal_level = jnp.where(quick, quick_rate, slow_rate)
    spike_occurred = jax.random.uniform(generator_seeds[3], (SEQUENCE_LENGTH, LATENT_FEATURES)) < 1.5 / SEQUENCE_LENGTH
    spike_sample = jnp.where(spike_occurred, jax.random.uniform(generator_seeds[4], (SEQUENCE_LENGTH, LATENT_FEATURES), jnp.float32, 0.5, 0.8), 1.0)
    small_perturbation = jnp.where(quick[None, :], jax.random.uniform(generator_seeds[5], (SEQUENCE_LENGTH, LATENT_FEATURES), jnp.float32, 0.6, 1.0), 1.0)
    return (nominal_level[None, :] * spike_sample * small_perturbation).astype(jnp.float32)


def steps_of(rng, shape, cuts, low, largest):
    gain, own = 1.0, jax.random.fold_in(rng, 6)
    for axis_at, blocks in cuts:
        steps = jnp.exp(jax.random.uniform(jax.random.fold_in(own, axis_at), (blocks,), jnp.float32, low / len(cuts), largest / len(cuts)))
        gain = gain * jnp.repeat(steps, shape[axis_at] // blocks).reshape([-1 if axis == axis_at else 1 for axis in range(len(shape))])
    return gain


def noise(stream_key, shape, deviation, limit, shards=(), dtype=jnp.bfloat16):
    entries = deviation * jax.random.normal(stream_key, shape, jnp.float32)
    if shards:
        entries = entries * steps_of(stream_key, shape, shards, -0.22, 0.18)
    return jnp.clip(entries, -limit, limit).astype(dtype)


def setup_inputs(seed: int = 0) -> dict:
    seeds = jax.random.split(jax.random.key(seed), 5)
    frames = noise(seeds[0], (SEQUENCE_LENGTH, HEIGHT, WIDTH, FEAT), 1.0, 6.0, ((0, 8), (1, 8), (2, 8)))
    in_weight = noise(seeds[1], (3, 3, FEAT, LATENT_FEATURES), (9 * FEAT) ** -0.5, 0.1875)
    out_weight = noise(seeds[2], (3, 3, LATENT_FEATURES, FEAT), (9 * LATENT_FEATURES) ** -0.5, 0.1875)
    decays = draw_decays(jax.random.fold_in(seeds[4], 71), 0)
    return {"frames": frames, "in_weight": in_weight, "out_weight": out_weight, "decays": decays}


def convolve(picture, weight):
    return lax.conv_general_dilated(picture[None], weight, (1, 1), 'SAME', dimension_numbers=('NHWC', 'HWIO', 'NHWC'), preferred_element_type=jnp.float32)[0]

def reference(frames, in_weight, out_weight, decays):

    def advance(carried, inputs):
        picture, factors = inputs
        driven = convolve(picture, in_weight)
        carried = factors * carried + jnp.sqrt(1.0 - factors * factors) * driven
        mixed = convolve(carried.astype(jnp.bfloat16), out_weight)
        result = (picture.astype(jnp.float32) + jax.nn.gelu(mixed)).astype(jnp.bfloat16)
        return (carried, result)
    initial = jnp.zeros((HEIGHT, WIDTH, LATENT_FEATURES), jnp.float32)
    return lax.scan(advance, initial, (frames, decays))[1]
```

```python
import functools

import jax
import jax.numpy as jnp
from jax import lax
from jax.experimental import pallas as pl
from jax.experimental.pallas import tpu as pltpu
from jax.sharding import PartitionSpec as P

MESH = pl.DeviceIdType.MESH
PAD = 8
F32 = jnp.float32
BF16 = jnp.bfloat16


def both(a, b):
    return jnp.logical_and(a, b)


def banded(dst, src):
    chans = src.shape[2]
    wide = src.shape[3]
    for i in range(4):
        for b in range(3):
            for o in range(2):
                at = (pl.ds(i * chans, chans), pl.ds((2 * b + o) * wide, wide))
                tap = i - o
                dst[at] = src[tap, b] if 0 <= tap <= 2 else jnp.zeros((chans, wide), BF16)


def conv_pair(rows, w, first):
    steps, cols, chans = rows[0].shape
    flat = jnp.concatenate([row.reshape(steps * cols, chans) for row in rows], axis=1)
    depth = flat.shape[1]
    wide = w.shape[1] // 3

    def part(b):
        block = w[pl.ds(first * chans, depth), pl.ds(b * wide, wide)]
        return jnp.dot(flat, block, preferred_element_type=F32).reshape(steps, cols, wide)

    total = part(1)
    total = total + pltpu.roll(part(0), 1, 1)
    return total + pltpu.roll(part(2), cols - 1, 1)


def kernel(
    x_hbm, wi_ref, wo_ref, dec, out, xp, wi, wo, u, st, prod, cin, cout, cup, cdn,
    loc, col_s, col_r, row_s, row_r, ch_s, ch_r, up_s, up_r, dn_s, dn_r,
):
    steps, height, width, chans = x_hbm.shape
    cols = width + 2 * PAD
    ext = height + 2
    g, h, k = lax.axis_index("gx"), lax.axis_index("gy"), lax.axis_index("ta")
    up, dn = g > 0, g < lax.axis_size("gx") - 1
    lf, rt = h > 0, h < lax.axis_size("gy") - 1
    pv, nx = k > 0, k < lax.axis_size("ta") - 1

    bar = pltpu.get_barrier_semaphore()
    partners = [
        (lf, (g, h - 1, k)), (rt, (g, h + 1, k)), (up, (g - 1, h, k)), (dn, (g + 1, h, k)),
        (pv, (g, h, k - 1)), (nx, (g, h, k + 1)),
        (both(up, pv), (g - 1, h, k - 1)), (both(up, nx), (g - 1, h, k + 1)),
        (both(dn, pv), (g + 1, h, k - 1)), (both(dn, nx), (g + 1, h, k + 1)),
    ]
    for there, device in partners:

        @pl.when(there)
        def _(device=device):
            pl.semaphore_signal(bar, inc=1, device_id=device, device_id_type=MESH)

    own = pltpu.make_async_copy(
        x_hbm, xp.at[:, pl.ds(2, height), pl.ds(PAD, width), :], loc.at[0]
    )
    own.start()

    @pl.when(jnp.logical_not(up))
    def _():
        xp[:, 0:2] = jnp.zeros((steps, 2, cols, chans), BF16)

    @pl.when(jnp.logical_not(dn))
    def _():
        xp[:, height + 2 : height + 4] = jnp.zeros((steps, 2, cols, chans), BF16)

    @pl.when(jnp.logical_not(lf))
    def _():
        xp[:, 2 : height + 2, 0:PAD] = jnp.zeros((steps, height, PAD, chans), BF16)

    @pl.when(jnp.logical_not(rt))
    def _():
        xp[:, 2 : height + 2, cols - PAD : cols] = jnp.zeros((steps, height, PAD, chans), BF16)

    @pl.when(jnp.logical_not(pv))
    def _():
        cin[...] = jnp.zeros(cin.shape, BF16)

    @pl.when(jnp.logical_not(both(pv, up)))
    def _():
        cup[...] = jnp.zeros(cup.shape, BF16)

    @pl.when(jnp.logical_not(both(pv, dn)))
    def _():
        cdn[...] = jnp.zeros(cdn.shape, BF16)

    banded(wi, wi_ref)
    banded(wo, wo_ref)
    running = dec[0:1, :]
    prod[0:1, :] = running
    for t in range(1, steps):
        running = running * dec[t : t + 1, :]
        prod[t : t + 1, :] = running

    count = sum(there.astype(jnp.int32) for there, _ in partners)
    pl.semaphore_wait(bar, count)

    def remote(src, dst, ss, rs, device):
        return pltpu.make_async_remote_copy(
            src_ref=src, dst_ref=dst, send_sem=ss, recv_sem=rs, device_id=device, device_id_type=MESH
        )

    mid = pl.ds(2, height)
    to_lf = remote(
        x_hbm.at[:, :, pl.ds(0, PAD), :], xp.at[:, mid, pl.ds(cols - PAD, PAD), :],
        col_s.at[0], col_r.at[1], (g, h - 1, k),
    )
    to_rt = remote(
        x_hbm.at[:, :, pl.ds(width - PAD, PAD), :], xp.at[:, mid, pl.ds(0, PAD), :],
        col_s.at[1], col_r.at[0], (g, h + 1, k),
    )
    to_up = remote(
        xp.at[:, pl.ds(2, 2)], xp.at[:, pl.ds(height + 2, 2)], row_s.at[0], row_r.at[1], (g - 1, h, k)
    )
    to_dn = remote(
        xp.at[:, pl.ds(height, 2)], xp.at[:, pl.ds(0, 2)], row_s.at[1], row_r.at[0], (g + 1, h, k)
    )
    pl.when(lf)(to_lf.start)
    pl.when(rt)(to_rt.start)
    own.wait()
    pl.when(lf)(to_rt.wait_recv)
    pl.when(rt)(to_lf.wait_recv)
    pl.when(up)(to_up.start)
    pl.when(dn)(to_dn.start)

    def local_states(e, rows, first, add):
        y = conv_pair(rows, wi, first)
        for o in range(2):
            state = None
            for t in range(steps):
                decay = dec[t : t + 1, :]
                drive = jnp.sqrt(1.0 - decay * decay) * y[t, :, o * chans : (o + 1) * chans]
                state = drive if state is None else decay * state + drive
                u[e + o, t] = u[e + o, t] + state if add else state

    def chain_copy(e):
        return remote(cout.at[e], cin.at[e], ch_s.at[e], ch_r.at[e], (g, h, k + 1))

    def down_copy(e):
        i = e - height
        return remote(cout.at[e], cup.at[i], up_s.at[i], up_r.at[i], (g + 1, h, k + 1))

    def up_copy(e):
        return remote(cout.at[e], cdn.at[e], dn_s.at[e], dn_r.at[e], (g - 1, h, k + 1))

    def pass_on(e, extra):
        pl.when(pv)(chain_copy(e).wait_recv)

        @pl.when(nx)
        def _():
            carried = prod[steps - 1 : steps, :] * cin[e].astype(F32) + u[e, steps - 1]
            cout[e] = carried.astype(BF16)
            chain_copy(e).start()
            if extra is not None:
                pl.when(extra[0])(extra[1](e).start)

    def finish(e, carried):
        for t in range(steps):
            st[e, t] = (u[e, t] + prod[t : t + 1, :] * carried).astype(BF16)

    local_states(height, [xp[:, height], xp[:, height + 1]], 0, False)
    local_states(0, [xp[:, 2], xp[:, 3]], 2, False)

    def inner(i, _):
        e = 2 * i
        local_states(e, [xp[:, e + j] for j in range(4)], 0, False)
        return 0

    lax.fori_loop(1, height // 2, inner, 0)
    for e in (height, height + 1):
        pass_on(e, (dn, down_copy))
    for e in (0, 1):
        pass_on(e, (up, up_copy))

    def link(e, _):
        pass_on(e, None)
        finish(e, cin[e].astype(F32))
        return 0

    lax.fori_loop(2, height, link, 0)

    def trim(first, rows):
        @pl.when(jnp.logical_not(lf))
        def _():
            st[first : first + rows, :, 0:PAD] = jnp.zeros((rows, steps, PAD, chans), BF16)

        @pl.when(jnp.logical_not(rt))
        def _():
            st[first : first + rows, :, cols - PAD : cols] = jnp.zeros((rows, steps, PAD, chans), BF16)

    def mix(r):
        y = conv_pair([st[r + j] for j in range(4)], wo, 0)
        for o in range(2):
            mixed = y[:, PAD : PAD + width, o * chans : (o + 1) * chans]
            held = xp[:, r + o + 2].astype(F32)[:, PAD : PAD + width]
            out[:, r + o] = (held + jax.nn.gelu(mixed)).astype(BF16)

    trim(2, height - 2)

    def inner_out(i, _):
        mix(2 * i)
        return 0

    lax.fori_loop(1, height // 2 - 1, inner_out, 0)

    pl.when(up)(to_dn.wait_recv)
    local_states(0, [xp[:, 0], xp[:, 1]], 0, True)
    pl.when(dn)(to_up.wait_recv)
    local_states(height, [xp[:, height + 2], xp[:, height + 3]], 2, True)
    for e in (0, 1):
        pl.when(both(pv, up))(down_copy(height + e).wait_recv)
        finish(e, cin[e].astype(F32) + cup[e].astype(F32))
    for e in (0, 1):
        pl.when(both(pv, dn))(up_copy(e).wait_recv)
        finish(height + e, cin[height + e].astype(F32) + cdn[e].astype(F32))
    trim(0, 2)
    trim(height, 2)

    @pl.when(jnp.logical_not(up))
    def _():
        st[0] = jnp.zeros((steps, cols, chans), BF16)

    @pl.when(jnp.logical_not(dn))
    def _():
        st[ext - 1] = jnp.zeros((steps, cols, chans), BF16)

    mix(0)
    mix(height - 2)

    pl.when(lf)(to_lf.wait_send)
    pl.when(rt)(to_rt.wait_send)
    pl.when(up)(to_up.wait_send)
    pl.when(dn)(to_dn.wait_send)
    for e in (height, height + 1):
        pl.when(both(nx, dn))(down_copy(e).wait_send)
    for e in (0, 1):
        pl.when(both(nx, up))(up_copy(e).wait_send)

    @pl.when(nx)
    def _():
        def sent(e, _):
            chain_copy(e).wait_send()
            return 0

        lax.fori_loop(0, ext, sent, 0)


def on_device(frames, in_weight, out_weight, decays):
    steps, height, width, chans = frames.shape
    cols, ext = width + 2 * PAD, height + 2
    dma = pltpu.SemaphoreType.DMA
    vmem = pl.BlockSpec(memory_space=pltpu.VMEM)
    return pl.pallas_call(
        kernel,
        out_shape=jax.ShapeDtypeStruct(frames.shape, BF16),
        in_specs=[pl.BlockSpec(memory_space=pl.ANY), vmem, vmem, vmem],
        out_specs=vmem,
        scratch_shapes=[
            pltpu.VMEM((steps, height + 4, cols, chans), BF16),
            pltpu.VMEM((4 * chans, 6 * chans), BF16),
            pltpu.VMEM((4 * chans, 6 * chans), BF16),
            pltpu.VMEM((ext, steps, cols, chans), F32),
            pltpu.VMEM((ext, steps, cols, chans), BF16),
            pltpu.VMEM((steps, chans), F32),
            pltpu.VMEM((ext, cols, chans), BF16),
            pltpu.VMEM((ext, cols, chans), BF16),
            pltpu.VMEM((2, cols, chans), BF16),
            pltpu.VMEM((2, cols, chans), BF16),
            dma((1,)), dma((2,)), dma((2,)), dma((2,)), dma((2,)),
            dma((ext,)), dma((ext,)), dma((2,)), dma((2,)), dma((2,)), dma((2,)),
        ],
        compiler_params=pltpu.CompilerParams(
            collective_id=0, has_side_effects=True, vmem_limit_bytes=60 << 20
        ),
        name="layer",
    )(frames, in_weight, out_weight, decays)


def solution(mesh):
    placed = (P("ta", "gx", "gy", None), P(), P(), P("ta", None))
    return jax.shard_map(
        on_device, mesh=mesh, in_specs=placed, out_specs=P("ta", "gx", "gy", None), check_vma=False
    )
```

```python
import functools

import jax
import jax.numpy as jnp
from jax import lax
from jax.experimental import pallas as pl
from jax.experimental.pallas import tpu as pltpu
from jax.sharding import PartitionSpec as P

MESH = pl.DeviceIdType.MESH
PAD = 8
F32 = jnp.float32
BF16 = jnp.bfloat16


def both(a, b):
    return jnp.logical_and(a, b)


def banded(dst, src):
    chans = src.shape[2]
    wide = src.shape[3]
    for i in range(4):
        for b in range(3):
            for o in range(2):
                at = (pl.ds(i * chans, chans), pl.ds((2 * b + o) * wide, wide))
                tap = i - o
                dst[at] = src[tap, b] if 0 <= tap <= 2 else jnp.zeros((chans, wide), BF16)


def conv_pair(rows, w, first):
    steps, cols, chans = rows[0].shape
    flat = jnp.concatenate([row.reshape(steps * cols, chans) for row in rows], axis=1)
    depth = flat.shape[1]
    wide = w.shape[1] // 3

    def part(b):
        block = w[pl.ds(pl.multiple_of(first * chans, chans), depth), pl.ds(b * wide, wide)]
        return jnp.dot(flat, block, preferred_element_type=F32).reshape(steps, cols, wide)

    total = part(1)
    total = total + pltpu.roll(part(0), 1, 1)
    return total + pltpu.roll(part(2), cols - 1, 1)


def kernel(
    x_hbm, wi_hbm, wo_hbm, dec_hbm, out, xp, wi_ref, wo_ref, dec, wi, wo, u, st, prod, cin, cout, cx, rb, last,
    far_ok, far_sem, loc, col_s, col_r, row_s, row_r, ch_s, ch_r, bd_s, bd_r, pc_s, pc_r, rl_s, rl_r,
):
    steps, height, width, chans = x_hbm.shape
    cols = width + 2 * PAD
    ext = height + 2
    half = lax.axis_size("gx") // 2
    span = steps // half
    g, h, k = lax.axis_index("gx"), lax.axis_index("gy"), lax.axis_index("ta")
    up, dn = g > 0, g < 2 * half - 1
    lf, rt = h > 0, h < lax.axis_size("gy") - 1
    pv, nx = k > 0, k < lax.axis_size("ta") - 1
    low = g < half
    m = jnp.where(low, g, 2 * half - 1 - g)
    cross = m == half - 1
    inner, outer = jnp.where(low, g + 1, g - 1), jnp.where(low, g - 1, g + 1)
    has_outer = m > 0
    far = 2 * half - 1 - g
    up_near, dn_near = both(up, g != half), both(dn, g != half - 1)

    q = lax.axis_size("ta") // 2
    early = k < q

    def collector(at):
        return jnp.where(at < q, at + q, at)

    bar = pltpu.get_barrier_semaphore()
    signals = [
        (cross, (far, h, collector(k))), (both(cross, pv), (far, h, collector(k - 1))),
        (both(cross, early), (g, h, k + q)),
        (lf, (g, h - 1, k)), (rt, (g, h + 1, k)), (pv, (g, h, k - 1)),
        (has_outer, (outer, h, k)), (jnp.logical_not(cross), (inner, h, k)),
        (both(has_outer, pv), (outer, h, k - 1)), (both(pv, jnp.logical_not(cross)), (inner, h, k - 1)),
        (m < half - 2, (jnp.where(low, half - 1, half), h, k)),
    ]
    for there, device in signals:

        @pl.when(there)
        def _(device=device):
            pl.semaphore_signal(bar, inc=1, device_id=device, device_id_type=MESH)

    own = pltpu.make_async_copy(
        x_hbm, xp.at[:, pl.ds(2, height), pl.ds(PAD, width), :], loc.at[0]
    )
    own.start()
    loads = [
        pltpu.make_async_copy(src, dst, loc.at[i + 1])
        for i, (src, dst) in enumerate(((wi_hbm, wi_ref), (dec_hbm, dec), (wo_hbm, wo_ref)))
    ]
    for load in loads:
        load.start()

    @pl.when(jnp.logical_not(up))
    def _():
        xp[:, 0:2] = jnp.zeros((steps, 2, cols, chans), BF16)

    @pl.when(jnp.logical_not(dn))
    def _():
        xp[:, height + 2 : height + 4] = jnp.zeros((steps, 2, cols, chans), BF16)

    @pl.when(jnp.logical_not(lf))
    def _():
        xp[:, 2 : height + 2, 0:PAD] = jnp.zeros((steps, height, PAD, chans), BF16)

    @pl.when(jnp.logical_not(rt))
    def _():
        xp[:, 2 : height + 2, cols - PAD : cols] = jnp.zeros((steps, height, PAD, chans), BF16)

    @pl.when(jnp.logical_not(pv))
    def _():
        cin[...] = jnp.zeros(cin.shape, BF16)

    @pl.when(jnp.logical_not(both(pv, up)))
    def _():
        cx[0:2] = jnp.zeros((2, cols, chans), BF16)

    @pl.when(jnp.logical_not(both(pv, dn)))
    def _():
        cx[2:4] = jnp.zeros((2, cols, chans), BF16)

    def num(flag):
        return flag.astype(jnp.int32)

    count = num(lf) + num(rt) + (1 + num(nx)) * (num(has_outer) + num(jnp.logical_not(cross))) + num(nx)
    count = count + num(cross) * (half - 2) + num(both(cross, jnp.logical_not(early))) * (4 + num(nx))
    pl.semaphore_wait(bar, count)

    def tell_relays():
        for i in range(half - 1):
            pl.semaphore_signal(
                far_sem, inc=1, device_id=(jnp.where(low, i, 2 * half - 1 - i), h, k), device_id_type=MESH
            )

    @pl.when(both(cross, jnp.logical_not(early)))
    def _():
        pl.semaphore_signal(far_ok, inc=1, device_id=(g, h, k - q), device_id_type=MESH)
        tell_relays()

    def remote(src, dst, ss, rs, device):
        return pltpu.make_async_remote_copy(
            src_ref=src, dst_ref=dst, send_sem=ss, recv_sem=rs, device_id=device, device_id_type=MESH
        )

    mid = pl.ds(2, height)
    to_lf = remote(
        x_hbm.at[:, :, pl.ds(0, PAD), :], xp.at[:, mid, pl.ds(cols - PAD, PAD), :],
        col_s.at[0], col_r.at[1], (g, h - 1, k),
    )
    to_rt = remote(
        x_hbm.at[:, :, pl.ds(width - PAD, PAD), :], xp.at[:, mid, pl.ds(0, PAD), :],
        col_s.at[1], col_r.at[0], (g, h + 1, k),
    )
    to_up = remote(
        xp.at[:, pl.ds(2, 2)], xp.at[:, pl.ds(height + 2, 2)], row_s.at[0], row_r.at[1], (g - 1, h, k)
    )
    to_dn = remote(
        xp.at[:, pl.ds(height, 2)], xp.at[:, pl.ds(0, 2)], row_s.at[1], row_r.at[0], (g + 1, h, k)
    )
    leave, land = jnp.where(low, height, 2), jnp.where(low, 0, height + 2)

    def piece(i):
        return remote(
            xp.at[pl.ds(span * i, span), pl.ds(leave, 2)], rb, pc_s.at[i], rl_r.at[0],
            (jnp.where(low, i, 2 * half - 1 - i), h, k),
        )

    def landing(i, src, ss):
        return remote(
            src, xp.at[pl.ds(span * i, span), pl.ds(land, 2)], ss, pc_r.at[i],
            (jnp.where(low, half, half - 1), h, k),
        )

    direct = landing(half - 1, xp.at[pl.ds(span * (half - 1), span), pl.ds(leave, 2)], pc_s.at[half - 1])
    forward = landing(m, rb, rl_s.at[0])

    pl.when(lf)(to_lf.start)
    pl.when(rt)(to_rt.start)
    for load in loads:
        load.wait()
    banded(wi, wi_ref)
    banded(wo, wo_ref)
    running = dec[0:1, :]
    prod[0:1, :] = running
    for t in range(1, steps):
        running = running * dec[t : t + 1, :]
        prod[t : t + 1, :] = running
    own.wait()
    pl.when(lf)(to_rt.wait_recv)
    pl.when(rt)(to_lf.wait_recv)

    @pl.when(cross)
    def _():
        for i in range(half - 1):
            piece(i).start()

    @pl.when(both(cross, jnp.logical_not(early)))
    def _():
        direct.start()

    pl.when(up_near)(to_up.start)
    pl.when(dn_near)(to_dn.start)

    def local_states(e, rows, first, add):
        y = conv_pair(rows, wi, first)
        for o in range(2):
            state = None
            for t in range(steps):
                decay = dec[t : t + 1, :]
                drive = jnp.sqrt(1.0 - decay * decay) * y[t, :, o * chans : (o + 1) * chans]
                state = drive if state is None else decay * state + drive
                u[e + o, t] = u[e + o, t] + state if add else state
            if not add:
                last[e + o] = state

    def chain_copy(e):
        return remote(cout.at[e], cin.at[e], ch_s.at[e], ch_r.at[e], (g, h, k + 1))

    def down_copy(o):
        return remote(cout.at[height + o], cx.at[o], bd_s.at[o], bd_r.at[o], (g + 1, h, k + 1))

    def up_copy(o):
        return remote(cout.at[o], cx.at[2 + o], bd_s.at[2 + o], bd_r.at[2 + o], (g - 1, h, k + 1))

    def send_row(e, value):
        cout[e] = value.astype(BF16)
        chain_copy(e).start()

    def send_edge(e, o):
        pl.when(both(e == 0, up))(up_copy(o).start)
        pl.when(both(e > 0, dn))(down_copy(o).start)

    def finish(e, carried):
        for t in range(steps):
            st[e, t] = (u[e, t] + prod[t : t + 1, :] * carried).astype(BF16)

    def edge(i):
        return jnp.where((i == 0) == low, height, 0)

    def held_back(i):
        return both(both(cross, early), i == 0)

    head = jnp.logical_not(pv)

    def own_edge(i, _):
        e = edge(i)
        r = jnp.where(e == 0, 2, height)
        local_states(e, [xp[:, r], xp[:, r + 1]], jnp.where(e == 0, 2, 0), False)

        @pl.when(both(head, nx))
        def _():
            for o in range(2):
                send_row(e + o, last[e + o])
                pl.when(jnp.logical_not(held_back(i)))(lambda o=o: send_edge(e, o))

        return 0

    lax.fori_loop(0, 2, own_edge, 0)

    def own_inner(i, _):
        e = 2 * i
        local_states(e, [xp[:, e + j] for j in range(4)], 0, False)

        @pl.when(both(head, nx))
        def _():
            for o in range(2):
                send_row(e + o, last[e + o])

        return 0

    lax.fori_loop(1, height // 2, own_inner, 0)

    def add_halo(e):
        r = jnp.where(e == 0, 0, height + 2)
        local_states(e, [xp[:, r], xp[:, r + 1]], jnp.where(e == 0, 0, 2), True)

    def near_halo(i, _):
        e = edge(i)

        @pl.when(jnp.where(i == 0, jnp.logical_not(cross), has_outer))
        def _():
            s = jnp.where(e == 0, 0, 1)
            remote(
                xp.at[:, pl.ds(2, 2)], xp.at[:, pl.ds(0, 2)], row_s.at[0], row_r.at[s], (g, h, k)
            ).wait_recv()
            add_halo(e)

        return 0

    def near_halos():
        lax.fori_loop(0, 2, near_halo, 0)

    late = both(k >= q, jnp.logical_or(m != half - 2, k >= q + 2))
    pl.when(late)(near_halos)

    def relay():
        pl.semaphore_wait(far_sem, 1)
        piece(0).wait_recv()
        forward.start()

    pl.when(both(jnp.logical_not(cross), jnp.logical_not(early)))(relay)

    def pass_on(e):
        chain_copy(e).wait_recv()
        carried = cin[e].astype(F32)

        @pl.when(nx)
        def _():
            send_row(e, prod[steps - 1 : steps, :] * carried + last[e])

        return carried

    def link_edge(i, _):
        e = edge(i)
        for o in range(2):
            pass_on(e + o)

            @pl.when(both(nx, jnp.logical_not(held_back(i))))
            def _():
                send_edge(e, o)

        return 0

    def link(e, _):
        finish(e, pass_on(e))
        return 0

    @pl.when(pv)
    def _():
        lax.fori_loop(0, 2, link_edge, 0)
        lax.fori_loop(2, height, link, 0)

    @pl.when(head)
    def _():
        def plain(e, _):
            for t in range(steps):
                st[e, t] = u[e, t].astype(BF16)
            return 0

        lax.fori_loop(2, height, plain, 0)

    @pl.when(both(cross, early))
    def _():
        pl.semaphore_wait(far_ok, 1)
        direct.start()
        tell_relays()

        @pl.when(nx)
        def _():
            for o in range(2):
                send_edge(edge(0), o)

    pl.when(both(jnp.logical_not(cross), early))(relay)

    def trim(first, rows):
        @pl.when(jnp.logical_not(lf))
        def _():
            st[pl.ds(first, rows), :, 0:PAD] = jnp.zeros((rows, steps, PAD, chans), BF16)

        @pl.when(jnp.logical_not(rt))
        def _():
            st[pl.ds(first, rows), :, cols - PAD : cols] = jnp.zeros((rows, steps, PAD, chans), BF16)

    def mix(r):
        y = conv_pair([st[r + j] for j in range(4)], wo, 0)
        for o in range(2):
            mixed = y[:, PAD : PAD + width, o * chans : (o + 1) * chans]
            held = xp[:, r + o + 2].astype(F32)[:, PAD : PAD + width]
            out[:, r + o] = (held + jax.nn.gelu(mixed)).astype(BF16)

    trim(2, height - 2)

    def inner_out(i, _):
        mix(2 * i)
        return 0

    lax.fori_loop(1, height // 2 - 1, inner_out, 0)
    pl.when(jnp.logical_not(late))(near_halos)

    def edge_out(i, _):
        e = edge(1 - i)
        top = e == 0

        @pl.when(both(cross, i == 1))
        def _():
            for j in range(half):
                landing(j, rb, pc_s.at[0]).wait_recv()
            add_halo(e)

        s = jnp.where(top, 0, 2)
        for o in range(2):
            pl.when(both(pv, jnp.where(top, up, dn)))(
                remote(cout.at[0], cx.at[0], bd_s.at[0], bd_r.at[s + o], (g, h, k)).wait_recv
            )
            finish(e + o, cin[e + o].astype(F32) + cx[s + o].astype(F32))
        trim(e, 2)

        @pl.when(jnp.logical_not(jnp.where(top, up, dn)))
        def _():
            st[jnp.where(top, 0, ext - 1)] = jnp.zeros((steps, cols, chans), BF16)

        mix(jnp.where(top, 0, height - 2))
        return 0

    lax.fori_loop(0, 2, edge_out, 0)

    pl.when(lf)(to_lf.wait_send)
    pl.when(rt)(to_rt.wait_send)
    pl.when(up_near)(to_up.wait_send)
    pl.when(dn_near)(to_dn.wait_send)

    @pl.when(cross)
    def _():
        for i in range(half - 1):
            piece(i).wait_send()
        direct.wait_send()

    @pl.when(jnp.logical_not(cross))
    def _():
        forward.wait_send()

    for o in range(2):
        pl.when(both(nx, dn))(down_copy(o).wait_send)
        pl.when(both(nx, up))(up_copy(o).wait_send)

    @pl.when(nx)
    def _():
        def sent(e, _):
            chain_copy(e).wait_send()
            return 0

        lax.fori_loop(0, ext, sent, 0)


def on_device(frames, in_weight, out_weight, decays):
    steps, height, width, chans = frames.shape
    cols, ext = width + 2 * PAD, height + 2
    half = lax.axis_size("gx") // 2
    dma = pltpu.SemaphoreType.DMA
    flag = pltpu.SemaphoreType.REGULAR
    hbm = pl.BlockSpec(memory_space=pltpu.HBM)
    return pl.pallas_call(
        kernel,
        out_shape=jax.ShapeDtypeStruct(frames.shape, BF16),
        in_specs=[hbm, hbm, hbm, hbm],
        out_specs=pl.BlockSpec(memory_space=pltpu.VMEM),
        scratch_shapes=[
            pltpu.VMEM((steps, height + 4, cols, chans), BF16),
            pltpu.VMEM(in_weight.shape, BF16),
            pltpu.VMEM(out_weight.shape, BF16),
            pltpu.VMEM(decays.shape, F32),
            pltpu.VMEM((4 * chans, 6 * chans), BF16),
            pltpu.VMEM((4 * chans, 6 * chans), BF16),
            pltpu.VMEM((ext, steps, cols, chans), F32),
            pltpu.VMEM((ext, steps, cols, chans), BF16),
            pltpu.VMEM((steps, chans), F32),
            pltpu.VMEM((ext, cols, chans), BF16),
            pltpu.VMEM((ext, cols, chans), BF16),
            pltpu.VMEM((4, cols, chans), BF16),
            pltpu.VMEM((steps // half, 2, cols, chans), BF16),
            pltpu.VMEM((ext, cols, chans), F32),
            flag, flag, dma((4,)), dma((2,)), dma((2,)), dma((2,)), dma((2,)),
            dma((ext,)), dma((ext,)), dma((4,)), dma((4,)), dma((half,)), dma((half,)), dma((1,)), dma((1,)),
        ],
        compiler_params=pltpu.CompilerParams(
            collective_id=0, has_side_effects=True, vmem_limit_bytes=28 << 20
        ),
        name="layer",
    )(frames, in_weight, out_weight, decays)


def solution(mesh):
    placed = (P("ta", "gx", "gy", None), P(), P(), P("ta", None))
    return jax.shard_map(
        on_device, mesh=mesh, in_specs=placed, out_specs=P("ta", "gx", "gy", None), check_vma=False
    )
```

```python
import functools

import jax
import jax.numpy as jnp
from jax import lax
from jax.experimental import pallas as pl
from jax.experimental.pallas import tpu as pltpu
from jax.sharding import PartitionSpec as P

MESH = pl.DeviceIdType.MESH
PAD = 4
F32 = jnp.float32
BF16 = jnp.bfloat16


def both(a, b):
    return jnp.logical_and(a, b)


def banded(dst, src):
    chans = src.shape[2]
    wide = src.shape[3]
    for i in range(4):
        for b in range(3):
            for o in range(2):
                at = (pl.ds(i * chans, chans), pl.ds((2 * b + o) * wide, wide))
                tap = i - o
                dst[at] = src[tap, b] if 0 <= tap <= 2 else jnp.zeros((chans, wide), BF16)


def conv_pair(rows, w, first):
    steps, cols, chans = rows[0].shape
    flat = jnp.concatenate([row.reshape(steps * cols, chans) for row in rows], axis=1)
    depth = flat.shape[1]
    wide = w.shape[1] // 3

    def part(b):
        block = w[pl.ds(pl.multiple_of(first * chans, chans), depth), pl.ds(b * wide, wide)]
        return jnp.dot(flat, block, preferred_element_type=F32).reshape(steps, cols, wide)

    total = part(1)
    total = total + pltpu.roll(part(0), 1, 1)
    return total + pltpu.roll(part(2), cols - 1, 1)


def kernel(
    x_hbm, wi_hbm, wo_hbm, dec_hbm, out, xp, wi_ref, wo_ref, dec, wi, wo, u, st, prod, cin, cout, cx, rb, last, cin2, cx2, before,
    far_ok, far_sem, loc, col_s, col_r, row_s, row_r, ch_s, ch_r, bd_s, bd_r, pc_s, pc_r, rl_s, rl_r,
    c2_s, c2_r, b2_s, b2_r, pr_s, pr_r,
):
    steps, height, width, chans = x_hbm.shape
    cols = width + 2 * PAD
    ext = height + 2
    half = lax.axis_size("gx") // 2
    span = steps // half
    g, h, k = lax.axis_index("gx"), lax.axis_index("gy"), lax.axis_index("ta")
    up, dn = g > 0, g < 2 * half - 1
    lf, rt = h > 0, h < lax.axis_size("gy") - 1
    pv, nx = k > 0, k < lax.axis_size("ta") - 1
    odd = lax.rem(k, 2) == 1
    even = jnp.logical_not(odd)
    pv2, nx2 = both(odd, k > 2), both(odd, k < lax.axis_size("ta") - 2)
    low = g < half
    m = jnp.where(low, g, 2 * half - 1 - g)
    cross = m == half - 1
    inner, outer = jnp.where(low, g + 1, g - 1), jnp.where(low, g - 1, g + 1)
    has_outer = m > 0
    far = 2 * half - 1 - g
    up_near, dn_near = both(up, g != half), both(dn, g != half - 1)

    q = lax.axis_size("ta") // 2
    early = k < q

    def collector(at):
        return jnp.where(at < q, at + q, at)

    bar = pltpu.get_barrier_semaphore()
    signals = [
        (cross, (far, h, collector(k))), (both(cross, pv), (far, h, collector(k - 1))),
        (both(cross, early), (g, h, k + q)),
        (lf, (g, h - 1, k)), (rt, (g, h + 1, k)), (pv, (g, h, k - 1)),
        (has_outer, (outer, h, k)), (jnp.logical_not(cross), (inner, h, k)),
        (both(has_outer, pv), (outer, h, k - 1)), (both(pv, jnp.logical_not(cross)), (inner, h, k - 1)),
        (m < half - 2, (jnp.where(low, half - 1, half), h, k)),
        (both(cross, pv2), (far, h, collector(k - 2))), (pv2, (g, h, k - 2)),
        (both(has_outer, pv2), (outer, h, k - 2)), (both(pv2, jnp.logical_not(cross)), (inner, h, k - 2)),
    ]
    for there, device in signals:

        @pl.when(there)
        def _(device=device):
            pl.semaphore_signal(bar, inc=1, device_id=device, device_id_type=MESH)

    own = pltpu.make_async_copy(
        x_hbm, xp.at[:, pl.ds(2, height), pl.ds(PAD, width), :], loc.at[0]
    )
    own.start()
    loads = [
        pltpu.make_async_copy(src, dst, loc.at[i + 1])
        for i, (src, dst) in enumerate(((wi_hbm, wi_ref), (dec_hbm, dec), (wo_hbm, wo_ref)))
    ]
    for load in loads:
        load.start()

    @pl.when(jnp.logical_not(up))
    def _():
        xp[:, 0:2] = jnp.zeros((steps, 2, cols, chans), BF16)

    @pl.when(jnp.logical_not(dn))
    def _():
        xp[:, height + 2 : height + 4] = jnp.zeros((steps, 2, cols, chans), BF16)

    @pl.when(jnp.logical_not(lf))
    def _():
        xp[:, 2 : height + 2, 0:PAD] = jnp.zeros((steps, height, PAD, chans), BF16)

    @pl.when(jnp.logical_not(rt))
    def _():
        xp[:, 2 : height + 2, cols - PAD : cols] = jnp.zeros((steps, height, PAD, chans), BF16)

    @pl.when(jnp.logical_not(pv))
    def _():
        cin[...] = jnp.zeros(cin.shape, BF16)

    @pl.when(jnp.logical_not(pv2))
    def _():
        cin2[...] = jnp.zeros(cin2.shape, BF16)
        before[...] = jnp.zeros(before.shape, F32)

    @pl.when(jnp.logical_not(both(pv2, up)))
    def _():
        cx2[0:2] = jnp.zeros((2, cols, chans), BF16)

    @pl.when(jnp.logical_not(both(pv2, dn)))
    def _():
        cx2[2:4] = jnp.zeros((2, cols, chans), BF16)

    @pl.when(jnp.logical_not(both(pv, up)))
    def _():
        cx[0:2] = jnp.zeros((2, cols, chans), BF16)

    @pl.when(jnp.logical_not(both(pv, dn)))
    def _():
        cx[2:4] = jnp.zeros((2, cols, chans), BF16)

    def num(flag):
        return flag.astype(jnp.int32)

    beside = num(has_outer) + num(jnp.logical_not(cross))
    count = num(lf) + num(rt) + beside + (num(nx) + num(nx2)) * (1 + beside) + num(cross) * (half - 2)
    second = num(nx2) + num(both(lax.rem(k + q, 2) == 1, k - q + 2 < 2 * q))
    count = count + num(both(cross, jnp.logical_not(early))) * (4 + num(nx) + second)
    pl.semaphore_wait(bar, count)

    def tell_relays():
        for i in range(half - 1):
            pl.semaphore_signal(
                far_sem, inc=1, device_id=(jnp.where(low, i, 2 * half - 1 - i), h, k), device_id_type=MESH
            )

    @pl.when(both(cross, jnp.logical_not(early)))
    def _():
        pl.semaphore_signal(far_ok, inc=1, device_id=(g, h, k - q), device_id_type=MESH)
        tell_relays()

    def remote(src, dst, ss, rs, device):
        return pltpu.make_async_remote_copy(
            src_ref=src, dst_ref=dst, send_sem=ss, recv_sem=rs, device_id=device, device_id_type=MESH
        )

    mid = pl.ds(2, height)
    to_lf = remote(
        x_hbm.at[:, :, pl.ds(0, PAD), :], xp.at[:, mid, pl.ds(cols - PAD, PAD), :],
        col_s.at[0], col_r.at[1], (g, h - 1, k),
    )
    to_rt = remote(
        x_hbm.at[:, :, pl.ds(width - PAD, PAD), :], xp.at[:, mid, pl.ds(0, PAD), :],
        col_s.at[1], col_r.at[0], (g, h + 1, k),
    )
    to_up = remote(
        xp.at[:, pl.ds(2, 2)], xp.at[:, pl.ds(height + 2, 2)], row_s.at[0], row_r.at[1], (g - 1, h, k)
    )
    to_dn = remote(
        xp.at[:, pl.ds(height, 2)], xp.at[:, pl.ds(0, 2)], row_s.at[1], row_r.at[0], (g + 1, h, k)
    )
    leave, land = jnp.where(low, height, 2), jnp.where(low, 0, height + 2)

    def piece(i):
        return remote(
            xp.at[pl.ds(span * i, span), pl.ds(leave, 2)], rb, pc_s.at[i], rl_r.at[0],
            (jnp.where(low, i, 2 * half - 1 - i), h, k),
        )

    def landing(i, src, ss):
        return remote(
            src, xp.at[pl.ds(span * i, span), pl.ds(land, 2)], ss, pc_r.at[i],
            (jnp.where(low, half, half - 1), h, k),
        )

    direct = landing(half - 1, xp.at[pl.ds(span * (half - 1), span), pl.ds(leave, 2)], pc_s.at[half - 1])
    forward = landing(m, rb, rl_s.at[0])

    pl.when(lf)(to_lf.start)
    pl.when(rt)(to_rt.start)
    for load in loads:
        load.wait()
    banded(wi, wi_ref)
    banded(wo, wo_ref)
    running = dec[0:1, :]
    prod[0:1, :] = running
    for t in range(1, steps):
        running = running * dec[t : t + 1, :]
        prod[t : t + 1, :] = running
    own.wait()
    pl.when(lf)(to_rt.wait_recv)
    pl.when(rt)(to_lf.wait_recv)

    @pl.when(cross)
    def _():
        for i in range(half - 1):
            piece(i).start()

    @pl.when(both(cross, jnp.logical_not(early)))
    def _():
        direct.start()

    pl.when(up_near)(to_up.start)
    pl.when(dn_near)(to_dn.start)

    def local_states(e, rows, first, add):
        y = conv_pair(rows, wi, first)
        for o in range(2):
            state = None
            for t in range(steps):
                decay = dec[t : t + 1, :]
                drive = jnp.sqrt(1.0 - decay * decay) * y[t, :, o * chans : (o + 1) * chans]
                state = drive if state is None else decay * state + drive
                u[e + o, t] = u[e + o, t] + state if add else state
            if not add:
                last[e + o] = state

    def chain_copy(e):
        return remote(cout.at[e], cin.at[e], ch_s.at[e], ch_r.at[e], (g, h, k + 1))

    def down_copy(o):
        return remote(cout.at[height + o], cx.at[o], bd_s.at[o], bd_r.at[o], (g + 1, h, k + 1))

    def up_copy(o):
        return remote(cout.at[o], cx.at[2 + o], bd_s.at[2 + o], bd_r.at[2 + o], (g - 1, h, k + 1))

    def chain_copy2(e):
        return remote(cout.at[e], cin2.at[e], c2_s.at[e], c2_r.at[e], (g, h, k + 2))

    def down_copy2(o):
        return remote(cout.at[height + o], cx2.at[o], b2_s.at[o], b2_r.at[o], (g + 1, h, k + 2))

    def up_copy2(o):
        return remote(cout.at[o], cx2.at[2 + o], b2_s.at[2 + o], b2_r.at[2 + o], (g - 1, h, k + 2))

    product = remote(prod, before, pr_s.at[0], pr_r.at[0], (g, h, k + 1))
    pl.when(both(even, both(pv, nx)))(product.start)

    def send_row(e, value):
        cout[e] = value.astype(BF16)
        pl.when(nx2)(chain_copy2(e).start)
        chain_copy(e).start()

    def send_edge(e, o):
        for there, first, second in ((both(e == 0, up), up_copy, up_copy2), (both(e > 0, dn), down_copy, down_copy2)):

            @pl.when(there)
            def _(first=first, second=second):
                pl.when(nx2)(second(o).start)
                first(o).start()

    def carry(e):
        return cin[e].astype(F32) + before[steps - 1 : steps, :] * cin2[e].astype(F32)

    def finish(e, carried):
        for t in range(steps):
            st[e, t] = (u[e, t] + prod[t : t + 1, :] * carried).astype(BF16)

    def edge(i):
        return jnp.where((i == 0) == low, height, 0)

    def held_back(i):
        return both(both(cross, both(early, k <= 2)), i == 0)


    def own_edge(i, _):
        e = edge(i)
        r = jnp.where(e == 0, 2, height)
        local_states(e, [xp[:, r], xp[:, r + 1]], jnp.where(e == 0, 2, 0), False)

        @pl.when(both(even, nx))
        def _():
            for o in range(2):
                send_row(e + o, last[e + o])
                pl.when(jnp.logical_not(held_back(i)))(lambda o=o: send_edge(e, o))

        return 0

    lax.fori_loop(0, 2, own_edge, 0)

    def own_inner(i, _):
        e = 2 * i
        local_states(e, [xp[:, e + j] for j in range(4)], 0, False)

        @pl.when(both(even, nx))
        def _():
            for o in range(2):
                send_row(e + o, last[e + o])

        return 0

    lax.fori_loop(1, height // 2, own_inner, 0)

    def add_halo(e):
        r = jnp.where(e == 0, 0, height + 2)
        local_states(e, [xp[:, r], xp[:, r + 1]], jnp.where(e == 0, 0, 2), True)

    def near_halo(i, _):
        e = edge(i)

        @pl.when(jnp.where(i == 0, jnp.logical_not(cross), has_outer))
        def _():
            s = jnp.where(e == 0, 0, 1)
            remote(
                xp.at[:, pl.ds(2, 2)], xp.at[:, pl.ds(0, 2)], row_s.at[0], row_r.at[s], (g, h, k)
            ).wait_recv()
            add_halo(e)

        return 0

    def near_halos():
        lax.fori_loop(0, 2, near_halo, 0)

    def far_ready():
        pl.semaphore_wait(far_ok, 1)
        direct.start()
        tell_relays()

        @pl.when(both(nx, k <= 2))
        def _():
            for o in range(2):
                send_edge(edge(0), o)

    def relay():
        pl.semaphore_wait(far_sem, 1)
        piece(0).wait_recv()
        forward.start()

    late = both(k >= q, jnp.logical_or(m != half - 2, k >= q + 2))
    pl.when(both(both(cross, early), k != 1))(far_ready)
    pl.when(late)(near_halos)
    pl.when(both(jnp.logical_not(cross), k != 1))(relay)
    pl.when(pv2)(product.wait_recv)

    def pass_on(e):
        chain_copy(e).wait_recv()
        pl.when(pv2)(chain_copy2(e).wait_recv)

        @pl.when(both(odd, nx))
        def _():
            send_row(e, prod[steps - 1 : steps, :] * carry(e) + last[e])

    def link_edge(i, _):
        e = edge(i)
        for o in range(2):
            pass_on(e + o)

            @pl.when(both(both(odd, nx), jnp.logical_not(held_back(i))))
            def _():
                send_edge(e, o)

        return 0

    @pl.when(pv)
    def _():
        lax.fori_loop(0, 2, link_edge, 0)

    def trim(first, rows):
        @pl.when(jnp.logical_not(lf))
        def _():
            st[pl.ds(first, rows), :, 0:PAD] = jnp.zeros((rows, steps, PAD, chans), BF16)

        @pl.when(jnp.logical_not(rt))
        def _():
            st[pl.ds(first, rows), :, cols - PAD : cols] = jnp.zeros((rows, steps, PAD, chans), BF16)

    def mix(r):
        y = conv_pair([st[r + j] for j in range(4)], wo, 0)
        for o in range(2):
            mixed = y[:, PAD : PAD + width, o * chans : (o + 1) * chans]
            held = xp[:, r + o + 2].astype(F32)[:, PAD : PAD + width]
            out[:, r + o] = (held + jax.nn.gelu(mixed)).astype(BF16)

    def first_row(j):
        return jnp.where(low, 2 * j, height - 2 - 2 * j)

    def inner_pair(j):
        e = first_row(j) + jnp.where(low, 2, 0)
        for o in range(2):
            pl.when(pv)(lambda o=o: pass_on(e + o))
            finish(e + o, carry(e + o))
        trim(e, 2)

    def edge_pair(i):
        e = edge(i)
        top = e == 0

        @pl.when(both(cross, i == 0))
        def _():
            for j in range(half):
                landing(j, rb, pc_s.at[0]).wait_recv()
            add_halo(e)

        s = jnp.where(top, 0, 2)
        for o in range(2):
            pl.when(both(pv, jnp.where(top, up, dn)))(
                remote(cout.at[0], cx.at[0], bd_s.at[0], bd_r.at[s + o], (g, h, k)).wait_recv
            )
            pl.when(both(pv2, jnp.where(top, up, dn)))(
                remote(cout.at[0], cx2.at[0], b2_s.at[0], b2_r.at[s + o], (g, h, k)).wait_recv
            )
            beyond = cx[s + o].astype(F32) + before[steps - 1 : steps, :] * cx2[s + o].astype(F32)
            finish(e + o, carry(e + o) + beyond)
        trim(e, 2)

        @pl.when(jnp.logical_not(jnp.where(top, up, dn)))
        def _():
            st[jnp.where(top, 0, ext - 1)] = jnp.zeros((steps, cols, chans), BF16)

    pairs = height // 2

    @pl.when(jnp.logical_not(late))
    def _():
        def one(j, _):
            inner_pair(j)
            return 0

        lax.fori_loop(0, pairs - 1, one, 0)

    pl.when(both(cross, k == 1))(far_ready)
    pl.when(both(jnp.logical_not(cross), k == 1))(relay)
    pl.when(jnp.logical_not(late))(near_halos)

    def row_pair(j, _):
        pl.when(both(late, j < pairs - 1))(lambda: inner_pair(j))
        pl.when(jnp.logical_or(j == 0, j == pairs - 1))(lambda: edge_pair(jnp.where(j == 0, 1, 0)))
        mix(first_row(j))
        return 0

    lax.fori_loop(0, pairs, row_pair, 0)

    pl.when(lf)(to_lf.wait_send)
    pl.when(rt)(to_rt.wait_send)
    pl.when(up_near)(to_up.wait_send)
    pl.when(dn_near)(to_dn.wait_send)

    @pl.when(cross)
    def _():
        for i in range(half - 1):
            piece(i).wait_send()
        direct.wait_send()

    @pl.when(jnp.logical_not(cross))
    def _():
        forward.wait_send()

    for o in range(2):
        pl.when(both(nx, dn))(down_copy(o).wait_send)
        pl.when(both(nx, up))(up_copy(o).wait_send)
        pl.when(both(nx2, dn))(down_copy2(o).wait_send)
        pl.when(both(nx2, up))(up_copy2(o).wait_send)
    pl.when(both(even, both(pv, nx)))(product.wait_send)

    @pl.when(nx)
    def _():
        def sent(e, _):
            chain_copy(e).wait_send()
            pl.when(nx2)(chain_copy2(e).wait_send)
            return 0

        lax.fori_loop(0, ext, sent, 0)


def on_device(frames, in_weight, out_weight, decays):
    steps, height, width, chans = frames.shape
    cols, ext = width + 2 * PAD, height + 2
    half = lax.axis_size("gx") // 2
    dma = pltpu.SemaphoreType.DMA
    flag = pltpu.SemaphoreType.REGULAR
    hbm = pl.BlockSpec(memory_space=pltpu.HBM)
    args = [
        pltpu.with_memory_space_constraint(arg, pltpu.HBM)
        for arg in (frames, in_weight, out_weight, decays)
    ]
    return pl.pallas_call(
        kernel,
        out_shape=jax.ShapeDtypeStruct(frames.shape, BF16),
        in_specs=[hbm, hbm, hbm, hbm],
        out_specs=pl.BlockSpec(memory_space=pltpu.VMEM),
        scratch_shapes=[
            pltpu.VMEM((steps, height + 4, cols, chans), BF16),
            pltpu.VMEM(in_weight.shape, BF16),
            pltpu.VMEM(out_weight.shape, BF16),
            pltpu.VMEM(decays.shape, F32),
            pltpu.VMEM((4 * chans, 6 * chans), BF16),
            pltpu.VMEM((4 * chans, 6 * chans), BF16),
            pltpu.VMEM((ext, steps, cols, chans), F32),
            pltpu.VMEM((ext, steps, cols, chans), BF16),
            pltpu.VMEM((steps, chans), F32),
            pltpu.VMEM((ext, cols, chans), BF16),
            pltpu.VMEM((ext, cols, chans), BF16),
            pltpu.VMEM((4, cols, chans), BF16),
            pltpu.VMEM((steps // half, 2, cols, chans), BF16),
            pltpu.VMEM((ext, cols, chans), F32),
            pltpu.VMEM((ext, cols, chans), BF16),
            pltpu.VMEM((4, cols, chans), BF16),
            pltpu.VMEM((steps, chans), F32),
            flag, flag, dma((4,)), dma((2,)), dma((2,)), dma((2,)), dma((2,)),
            dma((ext,)), dma((ext,)), dma((4,)), dma((4,)), dma((half,)), dma((half,)), dma((1,)), dma((1,)),
            dma((ext,)), dma((ext,)), dma((4,)), dma((4,)), dma((1,)), dma((1,)),
        ],
        compiler_params=pltpu.CompilerParams(
            collective_id=0, has_side_effects=True, vmem_limit_bytes=28 << 20
        ),
        name="layer",
    )(*args)


def solution(mesh):
    placed = (P("ta", "gx", "gy", None), P(), P(), P("ta", None))
    return jax.shard_map(
        on_device, mesh=mesh, in_specs=placed, out_specs=P("ta", "gx", "gy", None), check_vma=False
    )
```

```python
import functools

import jax
import jax.numpy as jnp
from jax import lax
from jax.experimental import pallas as pl
from jax.experimental.pallas import tpu as pltpu
from jax.sharding import PartitionSpec as P

MESH = pl.DeviceIdType.MESH
PAD = 4
F32 = jnp.float32
BF16 = jnp.bfloat16


def both(a, b):
    return jnp.logical_and(a, b)


def banded(dst, src):
    chans = src.shape[2]
    wide = src.shape[3]
    for i in range(4):
        for b in range(3):
            for o in range(2):
                at = (pl.ds(i * chans, chans), pl.ds((2 * b + o) * wide, wide))
                tap = i - o
                dst[at] = src[tap, b] if 0 <= tap <= 2 else jnp.zeros((chans, wide), BF16)


def conv_pair(rows, w, first):
    steps, cols, chans = rows[0].shape
    flat = jnp.concatenate([row.reshape(steps * cols, chans) for row in rows], axis=1)
    depth = flat.shape[1]
    wide = w.shape[1] // 3

    def part(b):
        block = w[pl.ds(pl.multiple_of(first * chans, chans), depth), pl.ds(b * wide, wide)]
        return jnp.dot(flat, block, preferred_element_type=F32).reshape(steps, cols, wide)

    total = part(1)
    total = total + pltpu.roll(part(0), 1, 1)
    return total + pltpu.roll(part(2), cols - 1, 1)


def kernel(
    x_hbm, wi_hbm, wo_hbm, dec_hbm, out, xp, wi_ref, wo_ref, dec, wi, wo, u, st, prod, cin, cout, cx, rb, last, cin2, cx2, before, cc,
    far_ok, far_sem, loc, col_s, col_r, row_s, row_r, ch_s, ch_r, bd_s, bd_r, pc_s, pc_r, rl_s, rl_r,
    c2_s, c2_r, b2_s, b2_r, pr_s, pr_r, nb_s,
):
    steps, height, width, chans = x_hbm.shape
    cols = width + 2 * PAD
    ext = height + 2
    half = lax.axis_size("gx") // 2
    span = steps // half
    g, h, k = lax.axis_index("gx"), lax.axis_index("gy"), lax.axis_index("ta")
    up, dn = g > 0, g < 2 * half - 1
    lf, rt = h > 0, h < lax.axis_size("gy") - 1
    pv, nx = k > 0, k < lax.axis_size("ta") - 1
    odd = lax.rem(k, 2) == 1
    even = jnp.logical_not(odd)
    pv2, nx2 = both(odd, k > 2), both(odd, k < lax.axis_size("ta") - 2)
    low = g < half
    m = jnp.where(low, g, 2 * half - 1 - g)
    cross = m == half - 1
    inner, outer = jnp.where(low, g + 1, g - 1), jnp.where(low, g - 1, g + 1)
    has_outer = m > 0
    far = 2 * half - 1 - g
    mine = jnp.where(low, half - 1, half)
    up_near, dn_near = both(up, g != half), both(dn, g != half - 1)

    q = lax.axis_size("ta") // 2
    early = k < q
    shifted = both(low, both(pv, early))
    here = jnp.logical_not(shifted)

    def collector(at):
        return jnp.where(at < q, at + q, at)

    bar = pltpu.get_barrier_semaphore()
    signals = [
        (cross, (far, h, collector(k))), (both(cross, pv), (far, h, collector(k - 1))),
        (both(cross, early), (g, h, k + q)),
        (lf, (g, h - 1, k)), (rt, (g, h + 1, k)), (pv, (g, h, k - 1)),
        (has_outer, (outer, h, k)), (jnp.logical_not(cross), (inner, h, k)),
        (both(m < half - 2, here), (mine, h, k)), (both(both(low, k < q - 1), jnp.logical_not(cross)), (mine, h, k + 1)),
        (both(cross, pv2), (far, h, collector(k - 2))), (pv2, (g, h, k - 2)),
    ]
    for there, device in signals:

        @pl.when(there)
        def _(device=device):
            pl.semaphore_signal(bar, inc=1, device_id=device, device_id_type=MESH)

    own = pltpu.make_async_copy(
        x_hbm, xp.at[:, pl.ds(2, height), pl.ds(PAD, width), :], loc.at[0]
    )
    own.start()
    loads = [
        pltpu.make_async_copy(src, dst, loc.at[i + 1])
        for i, (src, dst) in enumerate(((wi_hbm, wi_ref), (dec_hbm, dec), (wo_hbm, wo_ref)))
    ]
    for load in loads:
        load.start()

    @pl.when(jnp.logical_not(up))
    def _():
        xp[:, 0:2] = jnp.zeros((steps, 2, cols, chans), BF16)

    @pl.when(jnp.logical_not(dn))
    def _():
        xp[:, height + 2 : height + 4] = jnp.zeros((steps, 2, cols, chans), BF16)

    @pl.when(jnp.logical_not(lf))
    def _():
        xp[:, 2 : height + 2, 0:PAD] = jnp.zeros((steps, height, PAD, chans), BF16)

    @pl.when(jnp.logical_not(rt))
    def _():
        xp[:, 2 : height + 2, cols - PAD : cols] = jnp.zeros((steps, height, PAD, chans), BF16)

    @pl.when(jnp.logical_not(pv))
    def _():
        cin[...] = jnp.zeros(cin.shape, BF16)

    @pl.when(jnp.logical_not(pv2))
    def _():
        cin2[...] = jnp.zeros(cin2.shape, BF16)
        before[...] = jnp.zeros(before.shape, F32)

    @pl.when(jnp.logical_not(both(pv2, cross)))
    def _():
        cx2[...] = jnp.zeros(cx2.shape, BF16)

    @pl.when(both(pv2, cross))
    def _():
        cx2[pl.ds(jnp.where(low, 0, 2), 2)] = jnp.zeros((2, cols, chans), BF16)

    @pl.when(jnp.logical_not(both(pv, up)))
    def _():
        cx[0:2] = jnp.zeros((2, cols, chans), BF16)

    @pl.when(jnp.logical_not(both(pv, dn)))
    def _():
        cx[2:4] = jnp.zeros((2, cols, chans), BF16)

    def num(flag):
        return flag.astype(jnp.int32)

    beside = num(has_outer) + num(jnp.logical_not(cross))
    count = num(lf) + num(rt) + beside + num(nx) + num(nx2) + num(cross) * (half - 2 + num(shifted))
    second = num(nx2) + num(both(lax.rem(k + q, 2) == 1, k - q + 2 < 2 * q))
    count = count + num(both(cross, jnp.logical_not(early))) * (4 + num(nx) + second)
    pl.semaphore_wait(bar, count)

    slot, back = jnp.where(shifted, 0, 1), jnp.where(shifted, k - 1, k)

    def tell_relays():
        for i in range(half - 1):
            pl.semaphore_signal(
                far_sem.at[slot], inc=1, device_id=(jnp.where(low, i, 2 * half - 1 - i), h, back), device_id_type=MESH
            )

    @pl.when(both(cross, jnp.logical_not(early)))
    def _():
        pl.semaphore_signal(far_ok, inc=1, device_id=(g, h, k - q), device_id_type=MESH)
        tell_relays()

    def remote(src, dst, ss, rs, device):
        return pltpu.make_async_remote_copy(
            src_ref=src, dst_ref=dst, send_sem=ss, recv_sem=rs, device_id=device, device_id_type=MESH
        )

    mid = pl.ds(2, height)
    to_lf = remote(
        x_hbm.at[:, :, pl.ds(0, PAD), :], xp.at[:, mid, pl.ds(cols - PAD, PAD), :],
        col_s.at[0], col_r.at[1], (g, h - 1, k),
    )
    to_rt = remote(
        x_hbm.at[:, :, pl.ds(width - PAD, PAD), :], xp.at[:, mid, pl.ds(0, PAD), :],
        col_s.at[1], col_r.at[0], (g, h + 1, k),
    )
    to_up = remote(
        xp.at[:, pl.ds(2, 2)], xp.at[:, pl.ds(height + 2, 2)], row_s.at[0], row_r.at[1], (g - 1, h, k)
    )
    to_dn = remote(
        xp.at[:, pl.ds(height, 2)], xp.at[:, pl.ds(0, 2)], row_s.at[1], row_r.at[0], (g + 1, h, k)
    )
    leave, land = jnp.where(low, height, 2), jnp.where(low, 0, height + 2)

    def piece(i):
        return remote(
            xp.at[pl.ds(span * i, span), pl.ds(leave, 2)], rb.at[slot], pc_s.at[i], rl_r.at[slot],
            (jnp.where(low, i, 2 * half - 1 - i), h, back),
        )

    def landing(i, src, ss, at):
        return remote(
            src, xp.at[pl.ds(span * i, span), pl.ds(land, 2)], ss, pc_r.at[i],
            (jnp.where(low, half, half - 1), h, at),
        )

    direct = landing(half - 1, xp.at[pl.ds(span * (half - 1), span), pl.ds(leave, 2)], pc_s.at[half - 1], k)

    def forward(i):
        return landing(m, rb.at[i], rl_s.at[i], k + 1 - i)


    pl.when(lf)(to_lf.start)
    pl.when(rt)(to_rt.start)
    for load in loads:
        load.wait()
    banded(wi, wi_ref)
    banded(wo, wo_ref)
    running = dec[0:1, :]
    prod[0:1, :] = running
    for t in range(1, steps):
        running = running * dec[t : t + 1, :]
        prod[t : t + 1, :] = running
    own.wait()
    pl.when(lf)(to_rt.wait_recv)
    pl.when(rt)(to_lf.wait_recv)

    @pl.when(cross)
    def _():
        for i in range(half - 1):
            piece(i).start()

    @pl.when(both(cross, jnp.logical_not(early)))
    def _():
        direct.start()

    pl.when(up_near)(to_up.start)
    pl.when(dn_near)(to_dn.start)

    def local_states(e, rows, first, add):
        y = conv_pair(rows, wi, first)
        for o in range(2):
            state = None
            for t in range(steps):
                decay = dec[t : t + 1, :]
                drive = jnp.sqrt(1.0 - decay * decay) * y[t, :, o * chans : (o + 1) * chans]
                state = drive if state is None else decay * state + drive
                u[e + o, t] = u[e + o, t] + state if add else state
            if not add:
                last[e + o] = state

    def chain_copy(e):
        return remote(cout.at[e], cin.at[e], ch_s.at[e], ch_r.at[e], (g, h, k + 1))

    def chain_copy2(e):
        return remote(cout.at[e], cin2.at[e], c2_s.at[e], c2_r.at[e], (g, h, k + 2))

    def edge(i):
        return jnp.where((i == 0) == low, height, 0)

    theirs = jnp.where(low, 0, 2)

    def far_copy(o):
        return remote(
            cout.at[edge(0) + o], cx.at[theirs + o], bd_s.at[o], bd_r.at[theirs + o], (far, h, k + 1)
        )

    def far_copy2(o):
        return remote(
            cout.at[edge(0) + o], cx2.at[theirs + o], b2_s.at[o], b2_r.at[theirs + o], (far, h, k + 2)
        )

    def near_copy(i, o):
        top = edge(i) == 0
        there = jnp.where(top, 2, 0) + o
        return remote(
            cc.at[2 * i + o], cx.at[there], nb_s.at[2 * i + o], bd_r.at[there],
            (jnp.where(top, g - 1, g + 1), h, k),
        )

    def beside_at(i):
        return both(pv, jnp.where(i == 0, jnp.logical_not(cross), has_outer))

    product = remote(prod, before, pr_s.at[0], pr_r.at[0], (g, h, k + 1))
    pl.when(both(even, both(pv, nx)))(product.start)

    def send_row(e, value):
        cout[e] = value.astype(BF16)
        pl.when(nx2)(chain_copy2(e).start)
        chain_copy(e).start()

    def send_far(o):
        pl.when(nx2)(far_copy2(o).start)
        far_copy(o).start()

    def carry(e):
        return cin[e].astype(F32) + before[steps - 1 : steps, :] * cin2[e].astype(F32)

    def finish(e, carried):
        for t in range(steps):
            st[e, t] = (u[e, t] + prod[t : t + 1, :] * carried).astype(BF16)

    def far_now(i):
        waits = jnp.logical_or(both(early, both(even, k <= 2)), both(low, k == 1))
        return both(both(cross, jnp.logical_not(waits)), i == 0)


    def own_edge(i, _):
        e = edge(i)
        r = jnp.where(e == 0, 2, height)
        local_states(e, [xp[:, r], xp[:, r + 1]], jnp.where(e == 0, 2, 0), False)

        @pl.when(both(even, nx))
        def _():
            for o in range(2):
                send_row(e + o, last[e + o])
                pl.when(far_now(i))(lambda o=o: send_far(o))

        return 0

    lax.fori_loop(0, 2, own_edge, 0)

    def own_inner(i, _):
        e = 2 * i
        local_states(e, [xp[:, e + j] for j in range(4)], 0, False)

        @pl.when(both(even, nx))
        def _():
            for o in range(2):
                send_row(e + o, last[e + o])

        return 0

    lax.fori_loop(1, height // 2, own_inner, 0)

    def add_halo(e):
        r = jnp.where(e == 0, 0, height + 2)
        local_states(e, [xp[:, r], xp[:, r + 1]], jnp.where(e == 0, 0, 2), True)

    def near_halo(i, _):
        e = edge(i)

        @pl.when(jnp.where(i == 0, jnp.logical_not(cross), has_outer))
        def _():
            s = jnp.where(e == 0, 0, 1)
            remote(
                xp.at[:, pl.ds(2, 2)], xp.at[:, pl.ds(0, 2)], row_s.at[0], row_r.at[s], (g, h, k)
            ).wait_recv()
            add_halo(e)

        return 0

    def near_halos():
        lax.fori_loop(0, 2, near_halo, 0)

    def far_ready():
        pl.semaphore_wait(far_ok, 1)
        direct.start()
        tell_relays()

        @pl.when(both(nx, jnp.logical_or(both(even, k <= 2), wait_far)))
        def _():
            for o in range(2):
                send_far(o)

    def relay(i):
        pl.semaphore_wait(far_sem.at[i], 1)
        remote(
            xp.at[pl.ds(0, span), pl.ds(0, 2)], rb.at[i], pc_s.at[0], rl_r.at[i], (g, h, k)
        ).wait_recv()
        forward(i).start()

    late = both(k >= q, jnp.logical_or(m != half - 2, k >= q + 2))
    wait_far = both(k == 1, low)
    pl.when(both(both(cross, early), jnp.logical_not(wait_far)))(far_ready)
    pl.when(late)(near_halos)
    straight = jnp.logical_not(cross)
    pl.when(both(straight, both(here, k != 1)))(lambda: relay(1))
    serve = both(straight, both(low, k < q - 1))
    after = odd
    pl.when(both(serve, jnp.logical_not(after)))(lambda: relay(0))
    pl.when(pv2)(product.wait_recv)

    def pass_on(e):
        chain_copy(e).wait_recv()
        pl.when(pv2)(chain_copy2(e).wait_recv)

        @pl.when(both(odd, nx))
        def _():
            send_row(e, prod[steps - 1 : steps, :] * carry(e) + last[e])

    def link_edge(i, _):
        e = edge(i)
        for o in range(2):
            pass_on(e + o)

            pl.when(both(both(odd, nx), far_now(i)))(lambda o=o: send_far(o))

            @pl.when(beside_at(i))
            def _():
                cc[2 * i + o] = carry(e + o).astype(BF16)
                near_copy(i, o).start()

        return 0

    @pl.when(pv)
    def _():
        lax.fori_loop(0, 2, link_edge, 0)

    pl.when(both(straight, both(here, k == 1)))(lambda: relay(1))

    def trim(first, rows):
        @pl.when(jnp.logical_not(lf))
        def _():
            st[pl.ds(first, rows), :, 0:PAD] = jnp.zeros((rows, steps, PAD, chans), BF16)

        @pl.when(jnp.logical_not(rt))
        def _():
            st[pl.ds(first, rows), :, cols - PAD : cols] = jnp.zeros((rows, steps, PAD, chans), BF16)

    def mix(r):
        y = conv_pair([st[r + j] for j in range(4)], wo, 0)
        for o in range(2):
            mixed = y[:, PAD : PAD + width, o * chans : (o + 1) * chans]
            held = xp[:, r + o + 2].astype(F32)[:, PAD : PAD + width]
            out[:, r + o] = (held + jax.nn.gelu(mixed)).astype(BF16)

    def first_row(j):
        return jnp.where(low, 2 * j, height - 2 - 2 * j)

    def inner_pair(j):
        e = first_row(j) + jnp.where(low, 2, 0)
        for o in range(2):
            pl.when(pv)(lambda o=o: pass_on(e + o))
            finish(e + o, carry(e + o))
        trim(e, 2)

    def edge_pair(i):
        e = edge(i)
        top = e == 0

        @pl.when(both(cross, i == 0))
        def _():
            for j in range(half):
                landing(j, rb.at[0], pc_s.at[0], k).wait_recv()
            add_halo(e)

        s = jnp.where(top, 0, 2)
        for o in range(2):
            pl.when(both(pv, jnp.where(top, up, dn)))(
                remote(cout.at[0], cx.at[0], bd_s.at[0], bd_r.at[s + o], (g, h, k)).wait_recv
            )
            pl.when(both(pv2, both(cross, i == 0)))(
                remote(cout.at[0], cx2.at[0], b2_s.at[0], b2_r.at[s + o], (g, h, k)).wait_recv
            )
            beyond = cx[s + o].astype(F32) + before[steps - 1 : steps, :] * cx2[s + o].astype(F32)
            finish(e + o, carry(e + o) + beyond)
        trim(e, 2)

        @pl.when(jnp.logical_not(jnp.where(top, up, dn)))
        def _():
            st[jnp.where(top, 0, ext - 1)] = jnp.zeros((steps, cols, chans), BF16)

    pairs = height // 2

    @pl.when(jnp.logical_not(late))
    def _():
        def one(j, _):
            inner_pair(j)
            return 0

        lax.fori_loop(0, pairs - 1, one, 0)

    pl.when(both(cross, wait_far))(far_ready)
    pl.when(both(serve, after))(lambda: relay(0))
    pl.when(jnp.logical_not(late))(near_halos)

    def row_pair(j, _):
        pl.when(both(late, j < pairs - 1))(lambda: inner_pair(j))
        pl.when(jnp.logical_or(j == 0, j == pairs - 1))(lambda: edge_pair(jnp.where(j == 0, 1, 0)))
        mix(first_row(j))
        return 0

    lax.fori_loop(0, pairs, row_pair, 0)

    pl.when(lf)(to_lf.wait_send)
    pl.when(rt)(to_rt.wait_send)
    pl.when(up_near)(to_up.wait_send)
    pl.when(dn_near)(to_dn.wait_send)

    @pl.when(cross)
    def _():
        for i in range(half - 1):
            piece(i).wait_send()
        direct.wait_send()

    pl.when(serve)(lambda: forward(0).wait_send())
    pl.when(both(straight, here))(lambda: forward(1).wait_send())

    for o in range(2):
        pl.when(both(cross, nx))(far_copy(o).wait_send)
        pl.when(both(cross, nx2))(far_copy2(o).wait_send)
        for i in range(2):
            pl.when(beside_at(i))(near_copy(i, o).wait_send)
    pl.when(both(even, both(pv, nx)))(product.wait_send)

    @pl.when(nx)
    def _():
        def sent(e, _):
            chain_copy(e).wait_send()
            pl.when(nx2)(chain_copy2(e).wait_send)
            return 0

        lax.fori_loop(0, ext, sent, 0)


def on_device(frames, in_weight, out_weight, decays):
    steps, height, width, chans = frames.shape
    cols, ext = width + 2 * PAD, height + 2
    half = lax.axis_size("gx") // 2
    dma = pltpu.SemaphoreType.DMA
    flag = pltpu.SemaphoreType.REGULAR
    hbm = pl.BlockSpec(memory_space=pltpu.HBM)
    args = [
        pltpu.with_memory_space_constraint(arg, pltpu.HBM)
        for arg in (frames, in_weight, out_weight, decays)
    ]
    return pl.pallas_call(
        kernel,
        out_shape=jax.ShapeDtypeStruct(frames.shape, BF16),
        in_specs=[hbm, hbm, hbm, hbm],
        out_specs=pl.BlockSpec(memory_space=pltpu.VMEM),
        scratch_shapes=[
            pltpu.VMEM((steps, height + 4, cols, chans), BF16),
            pltpu.VMEM(in_weight.shape, BF16),
            pltpu.VMEM(out_weight.shape, BF16),
            pltpu.VMEM(decays.shape, F32),
            pltpu.VMEM((4 * chans, 6 * chans), BF16),
            pltpu.VMEM((4 * chans, 6 * chans), BF16),
            pltpu.VMEM((ext, steps, cols, chans), F32),
            pltpu.VMEM((ext, steps, cols, chans), BF16),
            pltpu.VMEM((steps, chans), F32),
            pltpu.VMEM((ext, cols, chans), BF16),
            pltpu.VMEM((ext, cols, chans), BF16),
            pltpu.VMEM((4, cols, chans), BF16),
            pltpu.VMEM((2, steps // half, 2, cols, chans), BF16),
            pltpu.VMEM((ext, cols, chans), F32),
            pltpu.VMEM((ext, cols, chans), BF16),
            pltpu.VMEM((4, cols, chans), BF16),
            pltpu.VMEM((steps, chans), F32),
            pltpu.VMEM((4, cols, chans), BF16),
            flag, pltpu.SemaphoreType.REGULAR((2,)), dma((4,)), dma((2,)), dma((2,)), dma((2,)), dma((2,)),
            dma((ext,)), dma((ext,)), dma((4,)), dma((4,)), dma((half,)), dma((half,)), dma((2,)), dma((2,)),
            dma((ext,)), dma((ext,)), dma((2,)), dma((4,)), dma((1,)), dma((1,)), dma((4,)),
        ],
        compiler_params=pltpu.CompilerParams(
            collective_id=0, has_side_effects=True, vmem_limit_bytes=28 << 20
        ),
        name="layer",
    )(*args)


def solution(mesh):
    placed = (P("ta", "gx", "gy", None), P(), P(), P("ta", None))
    return jax.shard_map(
        on_device, mesh=mesh, in_specs=placed, out_specs=P("ta", "gx", "gy", None), check_vma=False
    )
```

```python
import functools

import jax
import jax.numpy as jnp
from jax import lax
from jax.experimental import pallas as pl
from jax.experimental.pallas import tpu as pltpu
from jax.sharding import PartitionSpec as P

MESH = pl.DeviceIdType.MESH
PAD = 4
F32 = jnp.float32
BF16 = jnp.bfloat16


def both(a, b):
    return jnp.logical_and(a, b)


def banded(dst, src):
    chans = src.shape[2]
    wide = src.shape[3]
    for i in range(4):
        for b in range(3):
            for o in range(2):
                at = (pl.ds(i * chans, chans), pl.ds((2 * b + o) * wide, wide))
                tap = i - o
                dst[at] = src[tap, b] if 0 <= tap <= 2 else jnp.zeros((chans, wide), BF16)


def conv_pair(rows, w, first):
    steps, cols, chans = rows[0].shape
    flat = jnp.concatenate([row.reshape(steps * cols, chans) for row in rows], axis=1)
    depth = flat.shape[1]
    wide = w.shape[1] // 3

    def part(b):
        block = w[pl.ds(pl.multiple_of(first * chans, chans), depth), pl.ds(b * wide, wide)]
        return jnp.dot(flat, block, preferred_element_type=F32).reshape(steps, cols, wide)

    total = part(1)
    total = total + pltpu.roll(part(0), 1, 1)
    return total + pltpu.roll(part(2), cols - 1, 1)


def kernel(
    x_hbm, wi_hbm, wo_hbm, dec_hbm, out, xp, wi_ref, wo_ref, dec, wi, wo, u, st, prod, cin, cout, cx, rb, last, cin2, cx2, before, cc,
    far_ok, far_sem, loc, col_s, col_r, row_s, row_r, ch_s, ch_r, bd_s, bd_r, pc_s, pc_r, rl_s, rl_r,
    c2_s, c2_r, b2_s, b2_r, pr_s, pr_r, nb_s,
):
    steps, height, width, chans = x_hbm.shape
    cols = width + 2 * PAD
    ext = height + 2
    half = lax.axis_size("gx") // 2
    span = steps // half
    g, h, k = lax.axis_index("gx"), lax.axis_index("gy"), lax.axis_index("ta")
    up, dn = g > 0, g < 2 * half - 1
    lf, rt = h > 0, h < lax.axis_size("gy") - 1
    pv, nx = k > 0, k < lax.axis_size("ta") - 1
    odd = lax.rem(k, 2) == 1
    even = jnp.logical_not(odd)
    pv2, nx2 = both(odd, k > 2), both(odd, k < lax.axis_size("ta") - 2)
    low = g < half
    m = jnp.where(low, g, 2 * half - 1 - g)
    cross = m == half - 1
    inner, outer = jnp.where(low, g + 1, g - 1), jnp.where(low, g - 1, g + 1)
    has_outer = m > 0
    far = 2 * half - 1 - g
    mine = jnp.where(low, half - 1, half)
    up_near, dn_near = both(up, g != half), both(dn, g != half - 1)

    q = lax.axis_size("ta") // 2
    early = k < q
    shifted = both(low, both(pv, early))
    here = jnp.logical_not(shifted)

    def collector(at):
        return jnp.where(at < q, at + q, at)

    bar = pltpu.get_barrier_semaphore()
    signals = [
        (cross, (far, h, collector(k))), (both(cross, pv), (far, h, collector(k - 1))),
        (both(cross, early), (g, h, k + q)),
        (lf, (g, h - 1, k)), (rt, (g, h + 1, k)), (pv, (g, h, k - 1)),
        (has_outer, (outer, h, k)), (jnp.logical_not(cross), (inner, h, k)),
        (both(m < half - 2, here), (mine, h, k)), (both(both(low, k < q - 1), jnp.logical_not(cross)), (mine, h, k + 1)),
        (both(cross, pv2), (far, h, collector(k - 2))), (pv2, (g, h, k - 2)),
    ]
    for there, device in signals:

        @pl.when(there)
        def _(device=device):
            pl.semaphore_signal(bar, inc=1, device_id=device, device_id_type=MESH)

    own = pltpu.make_async_copy(
        x_hbm, xp.at[:, pl.ds(2, height), pl.ds(PAD, width), :], loc.at[0]
    )
    own.start()
    loads = [
        pltpu.make_async_copy(src, dst, loc.at[i + 1])
        for i, (src, dst) in enumerate(((wi_hbm, wi_ref), (dec_hbm, dec), (wo_hbm, wo_ref)))
    ]
    for load in loads:
        load.start()

    @pl.when(jnp.logical_not(up))
    def _():
        xp[:, 0:2] = jnp.zeros((steps, 2, cols, chans), BF16)

    @pl.when(jnp.logical_not(dn))
    def _():
        xp[:, height + 2 : height + 4] = jnp.zeros((steps, 2, cols, chans), BF16)

    @pl.when(jnp.logical_not(lf))
    def _():
        xp[:, 2 : height + 2, 0:PAD] = jnp.zeros((steps, height, PAD, chans), BF16)

    @pl.when(jnp.logical_not(rt))
    def _():
        xp[:, 2 : height + 2, cols - PAD : cols] = jnp.zeros((steps, height, PAD, chans), BF16)

    @pl.when(jnp.logical_not(pv))
    def _():
        cin[...] = jnp.zeros(cin.shape, BF16)

    @pl.when(jnp.logical_not(pv2))
    def _():
        cin2[...] = jnp.zeros(cin2.shape, BF16)
        before[...] = jnp.zeros(before.shape, F32)

    @pl.when(jnp.logical_not(both(pv2, cross)))
    def _():
        cx2[...] = jnp.zeros(cx2.shape, BF16)

    @pl.when(both(pv2, cross))
    def _():
        cx2[pl.ds(jnp.where(low, 0, 2), 2)] = jnp.zeros((2, cols, chans), BF16)

    @pl.when(jnp.logical_not(both(pv, up)))
    def _():
        cx[0:2] = jnp.zeros((2, cols, chans), BF16)

    @pl.when(jnp.logical_not(both(pv, dn)))
    def _():
        cx[2:4] = jnp.zeros((2, cols, chans), BF16)

    def num(flag):
        return flag.astype(jnp.int32)

    beside = num(has_outer) + num(jnp.logical_not(cross))
    count = num(lf) + num(rt) + beside + num(nx) + num(nx2) + num(cross) * (half - 2 + num(shifted))
    second = num(nx2) + num(both(lax.rem(k + q, 2) == 1, k - q + 2 < 2 * q))
    count = count + num(both(cross, jnp.logical_not(early))) * (4 + num(nx) + second)
    pl.semaphore_wait(bar, count)

    slot, back = jnp.where(shifted, 0, 1), jnp.where(shifted, k - 1, k)

    def tell_relays():
        for i in range(half - 1):
            pl.semaphore_signal(
                far_sem.at[slot], inc=1, device_id=(jnp.where(low, i, 2 * half - 1 - i), h, back), device_id_type=MESH
            )

    @pl.when(both(cross, jnp.logical_not(early)))
    def _():
        pl.semaphore_signal(far_ok, inc=1, device_id=(g, h, k - q), device_id_type=MESH)
        tell_relays()

    def remote(src, dst, ss, rs, device):
        return pltpu.make_async_remote_copy(
            src_ref=src, dst_ref=dst, send_sem=ss, recv_sem=rs, device_id=device, device_id_type=MESH
        )

    mid = pl.ds(2, height)
    to_lf = remote(
        x_hbm.at[:, :, pl.ds(0, PAD), :], xp.at[:, mid, pl.ds(cols - PAD, PAD), :],
        col_s.at[0], col_r.at[1], (g, h - 1, k),
    )
    to_rt = remote(
        x_hbm.at[:, :, pl.ds(width - PAD, PAD), :], xp.at[:, mid, pl.ds(0, PAD), :],
        col_s.at[1], col_r.at[0], (g, h + 1, k),
    )
    to_up = remote(
        xp.at[:, pl.ds(2, 2)], xp.at[:, pl.ds(height + 2, 2)], row_s.at[0], row_r.at[1], (g - 1, h, k)
    )
    to_dn = remote(
        xp.at[:, pl.ds(height, 2)], xp.at[:, pl.ds(0, 2)], row_s.at[1], row_r.at[0], (g + 1, h, k)
    )
    used = pl.ds(PAD - 2, width + 4)
    leave, land = jnp.where(low, height, 2), jnp.where(low, 0, height + 2)

    def piece(i):
        return remote(
            xp.at[pl.ds(span * i, span), pl.ds(leave, 2), used], rb.at[slot], pc_s.at[i], rl_r.at[slot],
            (jnp.where(low, i, 2 * half - 1 - i), h, back),
        )

    def landing(i, src, ss, at):
        return remote(
            src, xp.at[pl.ds(span * i, span), pl.ds(land, 2), used], ss, pc_r.at[i],
            (jnp.where(low, half, half - 1), h, at),
        )

    direct = landing(half - 1, xp.at[pl.ds(span * (half - 1), span), pl.ds(leave, 2), used], pc_s.at[half - 1], k)

    def forward(i):
        return landing(m, rb.at[i], rl_s.at[i], k + 1 - i)


    pl.when(lf)(to_lf.start)
    pl.when(rt)(to_rt.start)
    for load in loads:
        load.wait()
    banded(wi, wi_ref)
    banded(wo, wo_ref)
    running = dec[0:1, :]
    prod[0:1, :] = running
    for t in range(1, steps):
        running = running * dec[t : t + 1, :]
        prod[t : t + 1, :] = running
    own.wait()
    pl.when(lf)(to_rt.wait_recv)
    pl.when(rt)(to_lf.wait_recv)

    @pl.when(cross)
    def _():
        for i in range(half - 1):
            piece(i).start()

    @pl.when(both(cross, jnp.logical_not(early)))
    def _():
        direct.start()

    pl.when(up_near)(to_up.start)
    pl.when(dn_near)(to_dn.start)

    def local_states(e, rows, first, add):
        y = conv_pair(rows, wi, first)
        for o in range(2):
            state = None
            for t in range(steps):
                decay = dec[t : t + 1, :]
                drive = jnp.sqrt(1.0 - decay * decay) * y[t, :, o * chans : (o + 1) * chans]
                state = drive if state is None else decay * state + drive
                u[e + o, t] = u[e + o, t] + state if add else state
            if not add:
                last[e + o] = state

    def chain_copy(e):
        return remote(cout.at[e, used], cin.at[e, used], ch_s.at[e], ch_r.at[e], (g, h, k + 1))

    def chain_copy2(e):
        return remote(cout.at[e, used], cin2.at[e, used], c2_s.at[e], c2_r.at[e], (g, h, k + 2))

    def edge(i):
        return jnp.where((i == 0) == low, height, 0)

    theirs = jnp.where(low, 0, 2)

    def far_copy(o):
        return remote(
            cout.at[edge(0) + o], cx.at[theirs + o], bd_s.at[o], bd_r.at[theirs + o], (far, h, k + 1)
        )

    def far_copy2(o):
        return remote(
            cout.at[edge(0) + o], cx2.at[theirs + o], b2_s.at[o], b2_r.at[theirs + o], (far, h, k + 2)
        )

    def near_copy(i, o):
        top = edge(i) == 0
        there = jnp.where(top, 2, 0) + o
        return remote(
            cc.at[2 * i + o], cx.at[there], nb_s.at[2 * i + o], bd_r.at[there],
            (jnp.where(top, g - 1, g + 1), h, k),
        )

    def beside_at(i):
        return both(pv, jnp.where(i == 0, jnp.logical_not(cross), has_outer))

    product = remote(prod, before, pr_s.at[0], pr_r.at[0], (g, h, k + 1))
    pl.when(both(even, both(pv, nx)))(product.start)

    def send_row(e, value):
        cout[e] = value.astype(BF16)
        pl.when(nx2)(chain_copy2(e).start)
        chain_copy(e).start()

    def send_far(o):
        pl.when(nx2)(far_copy2(o).start)
        far_copy(o).start()

    def carry(e):
        return cin[e].astype(F32) + before[steps - 1 : steps, :] * cin2[e].astype(F32)

    def finish(e, carried):
        for t in range(steps):
            st[e, t] = (u[e, t] + prod[t : t + 1, :] * carried).astype(BF16)

    def far_now(i):
        waits = jnp.logical_or(both(early, both(even, k <= 2)), both(low, k == 1))
        return both(both(cross, jnp.logical_not(waits)), i == 0)


    def own_edge(i, _):
        e = edge(i)
        r = jnp.where(e == 0, 2, height)
        local_states(e, [xp[:, r], xp[:, r + 1]], jnp.where(e == 0, 2, 0), False)

        @pl.when(both(even, nx))
        def _():
            for o in range(2):
                send_row(e + o, last[e + o])
                pl.when(far_now(i))(lambda o=o: send_far(o))

        return 0

    lax.fori_loop(0, 2, own_edge, 0)

    def own_inner(i, _):
        e = 2 * i
        local_states(e, [xp[:, e + j] for j in range(4)], 0, False)

        @pl.when(both(even, nx))
        def _():
            for o in range(2):
                send_row(e + o, last[e + o])

        return 0

    lax.fori_loop(1, height // 2, own_inner, 0)

    def add_halo(e):
        r = jnp.where(e == 0, 0, height + 2)
        local_states(e, [xp[:, r], xp[:, r + 1]], jnp.where(e == 0, 0, 2), True)

    def near_halo(i, _):
        e = edge(i)

        @pl.when(jnp.where(i == 0, jnp.logical_not(cross), has_outer))
        def _():
            s = jnp.where(e == 0, 0, 1)
            remote(
                xp.at[:, pl.ds(2, 2)], xp.at[:, pl.ds(0, 2)], row_s.at[0], row_r.at[s], (g, h, k)
            ).wait_recv()
            add_halo(e)

        return 0

    def near_halos():
        lax.fori_loop(0, 2, near_halo, 0)

    def far_ready():
        pl.semaphore_wait(far_ok, 1)
        direct.start()
        tell_relays()

        @pl.when(both(nx, jnp.logical_or(both(even, k <= 2), wait_far)))
        def _():
            for o in range(2):
                send_far(o)

    def relay(i):
        pl.semaphore_wait(far_sem.at[i], 1)
        remote(
            xp.at[pl.ds(0, span), pl.ds(0, 2), used], rb.at[i], pc_s.at[0], rl_r.at[i], (g, h, k)
        ).wait_recv()
        forward(i).start()

    late = both(k >= q, jnp.logical_or(m != half - 2, k >= q + 2))
    wait_far = both(k == 1, low)
    pl.when(both(both(cross, early), jnp.logical_not(wait_far)))(far_ready)
    pl.when(late)(near_halos)
    straight = jnp.logical_not(cross)
    pl.when(both(straight, both(here, k != 1)))(lambda: relay(1))
    serve = both(straight, both(low, k < q - 1))
    after = odd
    pl.when(both(serve, jnp.logical_not(after)))(lambda: relay(0))
    pl.when(pv2)(product.wait_recv)

    def pass_on(e):
        chain_copy(e).wait_recv()
        pl.when(pv2)(chain_copy2(e).wait_recv)

        @pl.when(both(odd, nx))
        def _():
            send_row(e, prod[steps - 1 : steps, :] * carry(e) + last[e])

    def link_edge(i, _):
        e = edge(i)
        for o in range(2):
            pass_on(e + o)

            pl.when(both(both(odd, nx), far_now(i)))(lambda o=o: send_far(o))

            @pl.when(beside_at(i))
            def _():
                cc[2 * i + o] = carry(e + o).astype(BF16)
                near_copy(i, o).start()

        return 0

    @pl.when(pv)
    def _():
        lax.fori_loop(0, 2, link_edge, 0)

    pl.when(both(straight, both(here, k == 1)))(lambda: relay(1))

    def trim(first, rows):
        @pl.when(jnp.logical_not(lf))
        def _():
            st[pl.ds(first, rows), :, 0:PAD] = jnp.zeros((rows, steps, PAD, chans), BF16)

        @pl.when(jnp.logical_not(rt))
        def _():
            st[pl.ds(first, rows), :, cols - PAD : cols] = jnp.zeros((rows, steps, PAD, chans), BF16)

    def mix(r):
        y = conv_pair([st[r + j] for j in range(4)], wo, 0)
        for o in range(2):
            mixed = y[:, PAD : PAD + width, o * chans : (o + 1) * chans]
            held = xp[:, r + o + 2].astype(F32)[:, PAD : PAD + width]
            out[:, r + o] = (held + jax.nn.gelu(mixed)).astype(BF16)

    def first_row(j):
        return jnp.where(low, 2 * j, height - 2 - 2 * j)

    def inner_pair(j):
        e = first_row(j) + jnp.where(low, 2, 0)
        for o in range(2):
            pl.when(pv)(lambda o=o: pass_on(e + o))
            finish(e + o, carry(e + o))
        trim(e, 2)

    def edge_pair(i):
        e = edge(i)
        top = e == 0

        @pl.when(both(cross, i == 0))
        def _():
            for j in range(half):
                landing(j, rb.at[0], pc_s.at[0], k).wait_recv()
            add_halo(e)

        s = jnp.where(top, 0, 2)
        for o in range(2):
            pl.when(both(pv, jnp.where(top, up, dn)))(
                remote(cout.at[0], cx.at[0], bd_s.at[0], bd_r.at[s + o], (g, h, k)).wait_recv
            )
            pl.when(both(pv2, both(cross, i == 0)))(
                remote(cout.at[0], cx2.at[0], b2_s.at[0], b2_r.at[s + o], (g, h, k)).wait_recv
            )
            beyond = cx[s + o].astype(F32) + before[steps - 1 : steps, :] * cx2[s + o].astype(F32)
            finish(e + o, carry(e + o) + beyond)
        trim(e, 2)

        @pl.when(jnp.logical_not(jnp.where(top, up, dn)))
        def _():
            st[jnp.where(top, 0, ext - 1)] = jnp.zeros((steps, cols, chans), BF16)

    pairs = height // 2

    @pl.when(jnp.logical_not(late))
    def _():
        def one(j, _):
            inner_pair(j)
            return 0

        lax.fori_loop(0, pairs - 1, one, 0)

    pl.when(both(cross, wait_far))(far_ready)
    pl.when(both(serve, after))(lambda: relay(0))
    pl.when(jnp.logical_not(late))(near_halos)

    def row_pair(j, _):
        pl.when(both(late, j < pairs - 1))(lambda: inner_pair(j))
        pl.when(jnp.logical_or(j == 0, j == pairs - 1))(lambda: edge_pair(jnp.where(j == 0, 1, 0)))
        mix(first_row(j))
        return 0

    lax.fori_loop(0, pairs, row_pair, 0)

    pl.when(lf)(to_lf.wait_send)
    pl.when(rt)(to_rt.wait_send)
    pl.when(up_near)(to_up.wait_send)
    pl.when(dn_near)(to_dn.wait_send)

    @pl.when(cross)
    def _():
        for i in range(half - 1):
            piece(i).wait_send()
        direct.wait_send()

    pl.when(serve)(lambda: forward(0).wait_send())
    pl.when(both(straight, here))(lambda: forward(1).wait_send())

    for o in range(2):
        pl.when(both(cross, nx))(far_copy(o).wait_send)
        pl.when(both(cross, nx2))(far_copy2(o).wait_send)
        for i in range(2):
            pl.when(beside_at(i))(near_copy(i, o).wait_send)
    pl.when(both(even, both(pv, nx)))(product.wait_send)

    @pl.when(nx)
    def _():
        def sent(e, _):
            chain_copy(e).wait_send()
            pl.when(nx2)(chain_copy2(e).wait_send)
            return 0

        lax.fori_loop(0, ext, sent, 0)


def on_device(frames, in_weight, out_weight, decays):
    steps, height, width, chans = frames.shape
    cols, ext = width + 2 * PAD, height + 2
    half = lax.axis_size("gx") // 2
    dma = pltpu.SemaphoreType.DMA
    flag = pltpu.SemaphoreType.REGULAR
    hbm = pl.BlockSpec(memory_space=pltpu.HBM)
    args = [
        pltpu.with_memory_space_constraint(arg, pltpu.HBM)
        for arg in (frames, in_weight, out_weight, decays)
    ]
    return pl.pallas_call(
        kernel,
        out_shape=jax.ShapeDtypeStruct(frames.shape, BF16),
        in_specs=[hbm, hbm, hbm, hbm],
        out_specs=pl.BlockSpec(memory_space=pltpu.VMEM),
        scratch_shapes=[
            pltpu.VMEM((steps, height + 4, cols, chans), BF16),
            pltpu.VMEM(in_weight.shape, BF16),
            pltpu.VMEM(out_weight.shape, BF16),
            pltpu.VMEM(decays.shape, F32),
            pltpu.VMEM((4 * chans, 6 * chans), BF16),
            pltpu.VMEM((4 * chans, 6 * chans), BF16),
            pltpu.VMEM((ext, steps, cols, chans), F32),
            pltpu.VMEM((ext, steps, cols, chans), BF16),
            pltpu.VMEM((steps, chans), F32),
            pltpu.VMEM((ext, cols, chans), BF16),
            pltpu.VMEM((ext, cols, chans), BF16),
            pltpu.VMEM((4, cols, chans), BF16),
            pltpu.VMEM((2, steps // half, 2, width + 4, chans), BF16),
            pltpu.VMEM((ext, cols, chans), F32),
            pltpu.VMEM((ext, cols, chans), BF16),
            pltpu.VMEM((4, cols, chans), BF16),
            pltpu.VMEM((steps, chans), F32),
            pltpu.VMEM((4, cols, chans), BF16),
            flag, pltpu.SemaphoreType.REGULAR((2,)), dma((4,)), dma((2,)), dma((2,)), dma((2,)), dma((2,)),
            dma((ext,)), dma((ext,)), dma((4,)), dma((4,)), dma((half,)), dma((half,)), dma((2,)), dma((2,)),
            dma((ext,)), dma((ext,)), dma((2,)), dma((4,)), dma((1,)), dma((1,)), dma((4,)),
        ],
        compiler_params=pltpu.CompilerParams(
            collective_id=0, has_side_effects=True, vmem_limit_bytes=28 << 20
        ),
        name="layer",
    )(*args)


def solution(mesh):
    placed = (P("ta", "gx", "gy", None), P(), P(), P("ta", None))
    return jax.shard_map(
        on_device, mesh=mesh, in_specs=placed, out_specs=P("ta", "gx", "gy", None), check_vma=False
    )
```

```python
import functools

import jax
import jax.numpy as jnp
from jax import lax
from jax.experimental import pallas as pl
from jax.experimental.pallas import tpu as pltpu
from jax.sharding import PartitionSpec as P

MESH = pl.DeviceIdType.MESH
PAD = 4
F32 = jnp.float32
BF16 = jnp.bfloat16


def both(a, b):
    return jnp.logical_and(a, b)


def banded(dst, src):
    chans = src.shape[2]
    wide = src.shape[3]
    for i in range(4):
        for b in range(3):
            for o in range(2):
                at = (pl.ds(i * chans, chans), pl.ds((2 * b + o) * wide, wide))
                tap = i - o
                dst[at] = src[tap, b] if 0 <= tap <= 2 else jnp.zeros((chans, wide), BF16)


def conv_pair(rows, w, first):
    steps, cols, chans = rows[0].shape
    flat = jnp.concatenate([row.reshape(steps * cols, chans) for row in rows], axis=1)
    depth = flat.shape[1]
    wide = w.shape[1] // 3

    def part(b):
        block = w[pl.ds(pl.multiple_of(first * chans, chans), depth), pl.ds(b * wide, wide)]
        return jnp.dot(flat, block, preferred_element_type=F32).reshape(steps, cols, wide)

    total = part(1)
    total = total + pltpu.roll(part(0), 1, 1)
    return total + pltpu.roll(part(2), cols - 1, 1)


def kernel(
    x_hbm, wi_hbm, wo_hbm, dec_hbm, out, xp, wi_ref, wo_ref, dec, wi, wo, u, st, prod, cin, cout, cx, rb, last, cin2, cx2, before, cc,
    far_ok, far_sem, loc, col_s, col_r, row_s, row_r, ch_s, ch_r, bd_s, bd_r, pc_s, pc_r, rl_s, rl_r,
    c2_s, c2_r, b2_s, b2_r, pr_s, pr_r, nb_s,
):
    steps, height, width, chans = x_hbm.shape
    cols = width + 2 * PAD
    ext = height + 2
    half = lax.axis_size("gx") // 2
    span = steps // half
    g, h, k = lax.axis_index("gx"), lax.axis_index("gy"), lax.axis_index("ta")
    up, dn = g > 0, g < 2 * half - 1
    lf, rt = h > 0, h < lax.axis_size("gy") - 1
    pv, nx = k > 0, k < lax.axis_size("ta") - 1
    odd = lax.rem(k, 2) == 1
    even = jnp.logical_not(odd)
    pv2, nx2 = both(odd, k > 2), both(odd, k < lax.axis_size("ta") - 2)
    low = g < half
    m = jnp.where(low, g, 2 * half - 1 - g)
    cross = m == half - 1
    inner, outer = jnp.where(low, g + 1, g - 1), jnp.where(low, g - 1, g + 1)
    has_outer = m > 0
    far = 2 * half - 1 - g
    mine = jnp.where(low, half - 1, half)
    up_near, dn_near = both(up, g != half), both(dn, g != half - 1)

    q = lax.axis_size("ta") // 2
    early = k < q
    shifted = both(low, both(pv, early))
    here = jnp.logical_not(shifted)

    def collector(at):
        return jnp.where(at < q, at + q, at)

    bar = pltpu.get_barrier_semaphore()
    signals = [
        (cross, (far, h, collector(k))), (both(cross, pv), (far, h, collector(k - 1))),
        (both(cross, early), (g, h, k + q)),
        (lf, (g, h - 1, k)), (rt, (g, h + 1, k)), (pv, (g, h, k - 1)),
        (has_outer, (outer, h, k)), (jnp.logical_not(cross), (inner, h, k)),
        (both(m < half - 2, here), (mine, h, k)), (both(both(low, k < q - 1), jnp.logical_not(cross)), (mine, h, k + 1)),
        (both(cross, pv2), (far, h, collector(k - 2))), (pv2, (g, h, k - 2)),
    ]
    for there, device in signals:

        @pl.when(there)
        def _(device=device):
            pl.semaphore_signal(bar, inc=1, device_id=device, device_id_type=MESH)

    own = pltpu.make_async_copy(
        x_hbm, xp.at[:, pl.ds(2, height), pl.ds(PAD, width), :], loc.at[0]
    )
    own.start()
    loads = [
        pltpu.make_async_copy(src, dst, loc.at[i + 1])
        for i, (src, dst) in enumerate(((wi_hbm, wi_ref), (dec_hbm, dec), (wo_hbm, wo_ref)))
    ]
    for load in loads:
        load.start()

    @pl.when(jnp.logical_not(up))
    def _():
        xp[:, 0:2] = jnp.zeros((steps, 2, cols, chans), BF16)

    @pl.when(jnp.logical_not(dn))
    def _():
        xp[:, height + 2 : height + 4] = jnp.zeros((steps, 2, cols, chans), BF16)

    @pl.when(jnp.logical_not(lf))
    def _():
        xp[:, 2 : height + 2, 0:PAD] = jnp.zeros((steps, height, PAD, chans), BF16)

    @pl.when(jnp.logical_not(rt))
    def _():
        xp[:, 2 : height + 2, cols - PAD : cols] = jnp.zeros((steps, height, PAD, chans), BF16)

    @pl.when(jnp.logical_not(pv))
    def _():
        cin[...] = jnp.zeros(cin.shape, BF16)

    @pl.when(jnp.logical_not(pv2))
    def _():
        cin2[...] = jnp.zeros(cin2.shape, BF16)
        before[...] = jnp.zeros(before.shape, F32)

    @pl.when(jnp.logical_not(both(pv2, cross)))
    def _():
        cx2[...] = jnp.zeros(cx2.shape, BF16)

    @pl.when(both(pv2, cross))
    def _():
        cx2[pl.ds(jnp.where(low, 0, 2), 2)] = jnp.zeros((2, cols, chans), BF16)

    @pl.when(jnp.logical_not(both(pv, up)))
    def _():
        cx[0:2] = jnp.zeros((2, cols, chans), BF16)

    @pl.when(jnp.logical_not(both(pv, dn)))
    def _():
        cx[2:4] = jnp.zeros((2, cols, chans), BF16)

    def num(flag):
        return flag.astype(jnp.int32)

    beside = num(has_outer) + num(jnp.logical_not(cross))
    count = num(lf) + num(rt) + beside + num(nx) + num(nx2) + num(cross) * (half - 2 + num(shifted))
    second = num(nx2) + num(both(lax.rem(k + q, 2) == 1, k - q + 2 < 2 * q))
    count = count + num(both(cross, jnp.logical_not(early))) * (4 + num(nx) + second)
    pl.semaphore_wait(bar, count)

    slot, back = jnp.where(shifted, 0, 1), jnp.where(shifted, k - 1, k)

    def tell_relays():
        for i in range(half - 1):
            pl.semaphore_signal(
                far_sem.at[slot], inc=1, device_id=(jnp.where(low, i, 2 * half - 1 - i), h, back), device_id_type=MESH
            )

    @pl.when(both(cross, jnp.logical_not(early)))
    def _():
        pl.semaphore_signal(far_ok, inc=1, device_id=(g, h, k - q), device_id_type=MESH)
        tell_relays()

    def remote(src, dst, ss, rs, device):
        return pltpu.make_async_remote_copy(
            src_ref=src, dst_ref=dst, send_sem=ss, recv_sem=rs, device_id=device, device_id_type=MESH
        )

    mid = pl.ds(2, height)
    to_lf = remote(
        x_hbm.at[:, :, pl.ds(0, PAD), :], xp.at[:, mid, pl.ds(cols - PAD, PAD), :],
        col_s.at[0], col_r.at[1], (g, h - 1, k),
    )
    to_rt = remote(
        x_hbm.at[:, :, pl.ds(width - PAD, PAD), :], xp.at[:, mid, pl.ds(0, PAD), :],
        col_s.at[1], col_r.at[0], (g, h + 1, k),
    )
    to_up = remote(
        xp.at[:, pl.ds(2, 2)], xp.at[:, pl.ds(height + 2, 2)], row_s.at[0], row_r.at[1], (g - 1, h, k)
    )
    to_dn = remote(
        xp.at[:, pl.ds(height, 2)], xp.at[:, pl.ds(0, 2)], row_s.at[1], row_r.at[0], (g + 1, h, k)
    )
    used = pl.ds(PAD - 2, width + 4)
    leave, land = jnp.where(low, height, 2), jnp.where(low, 0, height + 2)

    def piece(i):
        return remote(
            xp.at[pl.ds(span * i, span), pl.ds(leave, 2), used], rb.at[slot], pc_s.at[i], rl_r.at[slot],
            (jnp.where(low, i, 2 * half - 1 - i), h, back),
        )

    def landing(i, src, ss, at):
        return remote(
            src, xp.at[pl.ds(span * i, span), pl.ds(land, 2), used], ss, pc_r.at[i],
            (jnp.where(low, half, half - 1), h, at),
        )

    direct = landing(half - 1, xp.at[pl.ds(span * (half - 1), span), pl.ds(leave, 2), used], pc_s.at[half - 1], k)

    def forward(i):
        return landing(m, rb.at[i], rl_s.at[i], k + 1 - i)


    pl.when(lf)(to_lf.start)
    pl.when(rt)(to_rt.start)
    for load in loads:
        load.wait()
    banded(wi, wi_ref)
    banded(wo, wo_ref)
    running = dec[0:1, :]
    prod[0:1, :] = running
    for t in range(1, steps):
        running = running * dec[t : t + 1, :]
        prod[t : t + 1, :] = running
    own.wait()
    pl.when(lf)(to_rt.wait_recv)
    pl.when(rt)(to_lf.wait_recv)

    @pl.when(cross)
    def _():
        for i in range(half - 1):
            piece(i).start()

    @pl.when(both(cross, jnp.logical_not(early)))
    def _():
        direct.start()

    pl.when(up_near)(to_up.start)
    pl.when(dn_near)(to_dn.start)

    def local_states(e, rows, first, add):
        y = conv_pair(rows, wi, first)
        for o in range(2):
            state = None
            for t in range(steps):
                decay = dec[t : t + 1, :]
                drive = jnp.sqrt(1.0 - decay * decay) * y[t, :, o * chans : (o + 1) * chans]
                state = drive if state is None else decay * state + drive
                u[e + o, t] = u[e + o, t] + state if add else state
            if not add:
                last[e + o] = state

    def chain_copy(e):
        return remote(cout.at[e, used], cin.at[e, used], ch_s.at[e], ch_r.at[e], (g, h, k + 1))

    def chain_copy2(e):
        return remote(cout.at[e, used], cin2.at[e, used], c2_s.at[e], c2_r.at[e], (g, h, k + 2))

    def edge(i):
        return jnp.where((i == 0) == low, height, 0)

    theirs = jnp.where(low, 0, 2)

    def far_copy(o):
        return remote(
            cout.at[edge(0) + o, used], cx.at[theirs + o, used], bd_s.at[o], bd_r.at[theirs + o], (far, h, k + 1)
        )

    def far_copy2(o):
        return remote(
            cout.at[edge(0) + o, used], cx2.at[theirs + o, used], b2_s.at[o], b2_r.at[theirs + o], (far, h, k + 2)
        )

    def near_copy(i, o):
        top = edge(i) == 0
        there = jnp.where(top, 2, 0) + o
        return remote(
            cc.at[2 * i + o, used], cx.at[there, used], nb_s.at[2 * i + o], bd_r.at[there],
            (jnp.where(top, g - 1, g + 1), h, k),
        )

    def beside_at(i):
        return both(pv, jnp.where(i == 0, jnp.logical_not(cross), has_outer))

    product = remote(prod, before, pr_s.at[0], pr_r.at[0], (g, h, k + 1))
    pl.when(both(even, both(pv, nx)))(product.start)

    def send_row(e, value):
        cout[e] = value.astype(BF16)
        pl.when(nx2)(chain_copy2(e).start)
        chain_copy(e).start()

    def send_far(o):
        pl.when(nx2)(far_copy2(o).start)
        far_copy(o).start()

    def carry(e):
        return cin[e].astype(F32) + before[steps - 1 : steps, :] * cin2[e].astype(F32)

    def finish(e, carried):
        for t in range(steps):
            st[e, t] = (u[e, t] + prod[t : t + 1, :] * carried).astype(BF16)

    def far_now(i):
        waits = jnp.logical_or(both(early, both(even, k <= 2)), both(low, k == 1))
        return both(both(cross, jnp.logical_not(waits)), i == 0)


    def own_edge(i, _):
        e = edge(i)
        r = jnp.where(e == 0, 2, height)
        local_states(e, [xp[:, r], xp[:, r + 1]], jnp.where(e == 0, 2, 0), False)

        @pl.when(both(even, nx))
        def _():
            for o in range(2):
                send_row(e + o, last[e + o])
                pl.when(far_now(i))(lambda o=o: send_far(o))

        return 0

    lax.fori_loop(0, 2, own_edge, 0)
    wait_far = both(k == 1, low)
    ahead = both(jnp.logical_not(low), both(early, pv))

    def far_ready():
        pl.semaphore_wait(far_ok, 1)
        direct.start()
        tell_relays()

        @pl.when(both(nx, jnp.logical_or(both(even, k <= 2), wait_far)))
        def _():
            for o in range(2):
                send_far(o)

    pl.when(both(cross, ahead))(far_ready)

    def own_inner(i, _):
        e = 2 * i
        local_states(e, [xp[:, e + j] for j in range(4)], 0, False)

        @pl.when(both(even, nx))
        def _():
            for o in range(2):
                send_row(e + o, last[e + o])

        return 0

    lax.fori_loop(1, height // 2, own_inner, 0)

    def add_halo(e):
        r = jnp.where(e == 0, 0, height + 2)
        local_states(e, [xp[:, r], xp[:, r + 1]], jnp.where(e == 0, 0, 2), True)

    def near_halo(i, _):
        e = edge(i)

        @pl.when(jnp.where(i == 0, jnp.logical_not(cross), has_outer))
        def _():
            s = jnp.where(e == 0, 0, 1)
            remote(
                xp.at[:, pl.ds(2, 2)], xp.at[:, pl.ds(0, 2)], row_s.at[0], row_r.at[s], (g, h, k)
            ).wait_recv()
            add_halo(e)

        return 0

    def near_halos():
        lax.fori_loop(0, 2, near_halo, 0)

    def relay(i):
        pl.semaphore_wait(far_sem.at[i], 1)
        remote(
            xp.at[pl.ds(0, span), pl.ds(0, 2), used], rb.at[i], pc_s.at[0], rl_r.at[i], (g, h, k)
        ).wait_recv()
        forward(i).start()

    late = both(k >= q, jnp.logical_or(m != half - 2, k >= q + 2))
    pl.when(both(both(cross, early), jnp.logical_not(jnp.logical_or(wait_far, ahead))))(far_ready)
    pl.when(late)(near_halos)
    straight = jnp.logical_not(cross)
    pl.when(both(straight, both(here, k != 1)))(lambda: relay(1))
    serve = both(straight, both(low, k < q - 1))
    after = odd
    pl.when(both(serve, jnp.logical_not(after)))(lambda: relay(0))
    pl.when(pv2)(product.wait_recv)

    def pass_on(e):
        chain_copy(e).wait_recv()
        pl.when(pv2)(chain_copy2(e).wait_recv)

        @pl.when(both(odd, nx))
        def _():
            send_row(e, prod[steps - 1 : steps, :] * carry(e) + last[e])

    def link_edge(i, _):
        e = edge(i)
        for o in range(2):
            pass_on(e + o)

            pl.when(both(both(odd, nx), far_now(i)))(lambda o=o: send_far(o))

            @pl.when(beside_at(i))
            def _():
                cc[2 * i + o] = carry(e + o).astype(BF16)
                near_copy(i, o).start()

        return 0

    @pl.when(pv)
    def _():
        lax.fori_loop(0, 2, link_edge, 0)

    pl.when(both(straight, both(here, k == 1)))(lambda: relay(1))

    def trim(first, rows):
        @pl.when(jnp.logical_not(lf))
        def _():
            st[pl.ds(first, rows), :, 0:PAD] = jnp.zeros((rows, steps, PAD, chans), BF16)

        @pl.when(jnp.logical_not(rt))
        def _():
            st[pl.ds(first, rows), :, cols - PAD : cols] = jnp.zeros((rows, steps, PAD, chans), BF16)

    def mix(r):
        y = conv_pair([st[r + j] for j in range(4)], wo, 0)
        for o in range(2):
            mixed = y[:, PAD : PAD + width, o * chans : (o + 1) * chans]
            held = xp[:, r + o + 2].astype(F32)[:, PAD : PAD + width]
            out[:, r + o] = (held + jax.nn.gelu(mixed)).astype(BF16)

    def first_row(j):
        return jnp.where(low, 2 * j, height - 2 - 2 * j)

    def inner_pair(j):
        e = first_row(j) + jnp.where(low, 2, 0)
        for o in range(2):
            pl.when(pv)(lambda o=o: pass_on(e + o))
            finish(e + o, carry(e + o))
        trim(e, 2)

    def edge_pair(i):
        e = edge(i)
        top = e == 0

        @pl.when(both(cross, i == 0))
        def _():
            for j in range(half):
                landing(j, rb.at[0], pc_s.at[0], k).wait_recv()
            add_halo(e)

        s = jnp.where(top, 0, 2)
        for o in range(2):
            pl.when(both(pv, jnp.where(top, up, dn)))(
                remote(cout.at[0, used], cx.at[0, used], bd_s.at[0], bd_r.at[s + o], (g, h, k)).wait_recv
            )
            pl.when(both(pv2, both(cross, i == 0)))(
                remote(cout.at[0, used], cx2.at[0, used], b2_s.at[0], b2_r.at[s + o], (g, h, k)).wait_recv
            )
            beyond = cx[s + o].astype(F32) + before[steps - 1 : steps, :] * cx2[s + o].astype(F32)
            finish(e + o, carry(e + o) + beyond)
        trim(e, 2)

        @pl.when(jnp.logical_not(jnp.where(top, up, dn)))
        def _():
            st[jnp.where(top, 0, ext - 1)] = jnp.zeros((steps, cols, chans), BF16)

    pairs = height // 2

    @pl.when(jnp.logical_not(late))
    def _():
        def one(j, _):
            inner_pair(j)
            return 0

        lax.fori_loop(0, pairs - 1, one, 0)

    pl.when(both(cross, wait_far))(far_ready)
    pl.when(both(serve, after))(lambda: relay(0))
    pl.when(jnp.logical_not(late))(near_halos)

    def row_pair(j, _):
        pl.when(both(late, j < pairs - 1))(lambda: inner_pair(j))
        pl.when(jnp.logical_or(j == 0, j == pairs - 1))(lambda: edge_pair(jnp.where(j == 0, 1, 0)))
        mix(first_row(j))
        return 0

    lax.fori_loop(0, pairs, row_pair, 0)

    pl.when(lf)(to_lf.wait_send)
    pl.when(rt)(to_rt.wait_send)
    pl.when(up_near)(to_up.wait_send)
    pl.when(dn_near)(to_dn.wait_send)

    @pl.when(cross)
    def _():
        for i in range(half - 1):
            piece(i).wait_send()
        direct.wait_send()

    pl.when(serve)(lambda: forward(0).wait_send())
    pl.when(both(straight, here))(lambda: forward(1).wait_send())

    for o in range(2):
        pl.when(both(cross, nx))(far_copy(o).wait_send)
        pl.when(both(cross, nx2))(far_copy2(o).wait_send)
        for i in range(2):
            pl.when(beside_at(i))(near_copy(i, o).wait_send)
    pl.when(both(even, both(pv, nx)))(product.wait_send)

    @pl.when(nx)
    def _():
        def sent(e, _):
            chain_copy(e).wait_send()
            pl.when(nx2)(chain_copy2(e).wait_send)
            return 0

        lax.fori_loop(0, ext, sent, 0)


def on_device(frames, in_weight, out_weight, decays):
    steps, height, width, chans = frames.shape
    cols, ext = width + 2 * PAD, height + 2
    half = lax.axis_size("gx") // 2
    dma = pltpu.SemaphoreType.DMA
    flag = pltpu.SemaphoreType.REGULAR
    hbm = pl.BlockSpec(memory_space=pltpu.HBM)
    args = [
        pltpu.with_memory_space_constraint(arg, pltpu.HBM)
        for arg in (frames, in_weight, out_weight, decays)
    ]
    return pl.pallas_call(
        kernel,
        out_shape=jax.ShapeDtypeStruct(frames.shape, BF16),
        in_specs=[hbm, hbm, hbm, hbm],
        out_specs=pl.BlockSpec(memory_space=pltpu.VMEM),
        scratch_shapes=[
            pltpu.VMEM((steps, height + 4, cols, chans), BF16),
            pltpu.VMEM(in_weight.shape, BF16),
            pltpu.VMEM(out_weight.shape, BF16),
            pltpu.VMEM(decays.shape, F32),
            pltpu.VMEM((4 * chans, 6 * chans), BF16),
            pltpu.VMEM((4 * chans, 6 * chans), BF16),
            pltpu.VMEM((ext, steps, cols, chans), F32),
            pltpu.VMEM((ext, steps, cols, chans), BF16),
            pltpu.VMEM((steps, chans), F32),
            pltpu.VMEM((ext, cols, chans), BF16),
            pltpu.VMEM((ext, cols, chans), BF16),
            pltpu.VMEM((4, cols, chans), BF16),
            pltpu.VMEM((2, steps // half, 2, width + 4, chans), BF16),
            pltpu.VMEM((ext, cols, chans), F32),
            pltpu.VMEM((ext, cols, chans), BF16),
            pltpu.VMEM((4, cols, chans), BF16),
            pltpu.VMEM((steps, chans), F32),
            pltpu.VMEM((4, cols, chans), BF16),
            flag, pltpu.SemaphoreType.REGULAR((2,)), dma((4,)), dma((2,)), dma((2,)), dma((2,)), dma((2,)),
            dma((ext,)), dma((ext,)), dma((4,)), dma((4,)), dma((half,)), dma((half,)), dma((2,)), dma((2,)),
            dma((ext,)), dma((ext,)), dma((2,)), dma((4,)), dma((1,)), dma((1,)), dma((4,)),
        ],
        compiler_params=pltpu.CompilerParams(
            collective_id=0, has_side_effects=True, vmem_limit_bytes=28 << 20
        ),
        name="layer",
    )(*args)


def solution(mesh):
    placed = (P("ta", "gx", "gy", None), P(), P(), P("ta", None))
    return jax.shard_map(
        on_device, mesh=mesh, in_specs=placed, out_specs=P("ta", "gx", "gy", None), check_vma=False
    )
```
